256 devices in a mesh: dp: 4 (over y), seq: 8 (over x, z_lo), tensor: 8 (over z_hi, core).
Axes of the slice: x: 4, y: 4, z: 8 (z_hi: 4, z_lo: 2; z = z_hi * 2 + z_lo), core: 2. Of those that a mesh axis runs over, the one named last changes fastest.
Arguments:
- inputs: bfloat16 [4096, 3584], P(('dp', 'seq'), 'tensor'), parts along dimension 0, may hold values from -6 to 6
- cotangent: bfloat16 [4096, 3584], P(('dp', 'seq'), 'tensor'), parts along dimension 0, may hold values from -6 to 6
- norm_gain: float32 [2, 3584], replicated, may hold values from 0.25 to 1.75
- head_gain: float32 [2, 2, 128], replicated, may hold values from 0.5 to 2.5
- query_weight: bfloat16 [2, 3584, 2048], P(None, None, 'tensor'), may hold values from -0.09375 to 0.09375
- key_weight: bfloat16 [2, 3584, 1024], P(None, None, 'tensor'), may hold values from -0.09375 to 0.09375
- output_weight: bfloat16 [2, 2048, 3584], P(None, 'tensor'), may hold values from -0.375 to 0.375
- modality: int32 [4096], P(('dp', 'seq')), parts along dimension 0, may hold values 0 or 1
- segments: int32 [4096], P('dp'), parts along dimension 0, may hold values from 0 to 127, never falling along the last dimension, each value on 1 to 256 neighbouring positions
- block_order: int32 [32], P('dp'), parts along dimension 0, may hold values from 0 to 7, each once
Outputs:
- attention_out: bfloat16 [4096, 3584], P(('dp', 'seq'), 'tensor'), parts along dimension 0
- grad_input: bfloat16 [4096, 3584], P(('dp', 'seq'), 'tensor'), parts along dimension 0
The draws below stay inside these ranges and needn't reach their ends.
There are 4 independent parts, one for each index of `dp`. The reference program is written for one: setup_inputs(seed, part) draws one part's arguments, and reference() takes and returns one part's arrays. A program takes and returns all parts, laid end to end along the dimension named above; an argument that names none is the same for every part. Nothing has to cross between parts.
Inputs may be any that keep to these rules, and one draw needn't show every extreme that they name: `modality`: 1 marks an image token, 0 a text token. `segments`: never falls along the sequence; each segment covers 1 to 256 positions and one covers exactly 256. `block_order`: each block appears once.
All inputs are finite; a program needn't handle non-finite values. No bound on the sum of `modality` on one device may be relied on, other than what follows from the above.
Results may differ from the reference program's by a relative error of at most 0.022.
Values may be sent and summed in bfloat16 or wider, within the bound.
A program may use at most 64 MiB of HBM per device.

```python
import math
import jax
import jax.numpy as jnp
import numpy as np
from jax import lax

D = 3584
HEADS = 16
KV_HEADS = 4
HEAD_DIM = 128
GROUP = 4
TOK_DEV = 128
TOKENS = 1024
BLOCKS = 8
SEGS = 128
SEG_MOST = 256


def place_ends(drawn, own_key, low, largest):
    extent = drawn.shape
    place = [jax.random.randint(jax.random.fold_in(own_key, axis), (), 0, extent[axis]) for axis in range(len(extent))]
    drawn = drawn.at[tuple(place)].set(low)
    longest = extent.index(max(extent))
    place[longest] = (place[longest] + 1) % extent[longest]
    return drawn.at[tuple(place)].set(largest)


def block_scale(rng, shape, pieces, low, largest):
    factor_of, own = 1.0, jax.random.fold_in(rng, 6)
    for position, parts in pieces:
        steps = jnp.exp(jax.random.uniform(jax.random.fold_in(own, position), (parts,), jnp.float32, low / len(pieces), largest / len(pieces)))
        factor_of = factor_of * jnp.repeat(steps, shape[position] // parts).reshape([-1 if axis == position else 1 for axis in range(len(shape))])
    return factor_of


def length_profile(number_of, total, most, slope):
    portions = [(1 << 20) // math.isqrt(rank ** slope) + 1 for rank in range(2, number_of + 1)]
    spare, given = total - most - (number_of - 1), [1] * (number_of - 1)
    while spare > 0:
        candidates = [i for i in range(number_of - 1) if given[i] < most]
        pool, left = sum([portions[i] for i in candidates]), spare
        for i in candidates:
            more = min(most - given[i], max(1, left * portions[i] // pool), spare)
            given[i] = given[i] + more
            spare = spare - more
    return np.array([most] + given)


def uneven(stream_key, number_of, total, most, lean):
    if number_of == 2:
        one = jax.random.randint(stream_key, (), max(1, total - most), min(most, total - 1) + 1)
        return jnp.stack([one, total - one])
    sizes = jnp.asarray(length_profile(number_of, total, most, lean), jnp.int32)
    pairs = (number_of - 1) // 2
    donor, receiver = sizes[1:1 + 2 * pairs:2], sizes[2:2 + 2 * pairs:2]
    margin = jnp.minimum(donor - 1, most - receiver)
    passed = jax.random.randint(jax.random.fold_in(stream_key, 1), (pairs,), 0, 1 << 20) % (margin + 1)
    sizes = sizes.at[1:1 + 2 * pairs:2].set(donor - passed).at[2:2 + 2 * pairs:2].set(receiver + passed)
    return sizes[jax.random.permutation(jax.random.fold_in(stream_key, 2), number_of)]


def centred(stream_key, shape, width, most, split=(), kind=jnp.bfloat16):
    drawn = jax.random.normal(stream_key, shape, jnp.float32) * width
    if len(split) > 0:
        drawn = block_scale(stream_key, shape, split, -0.22, 0.18) * drawn
    return jnp.clip(drawn, min=-most, max=most).astype(kind)


def setup_inputs(seed: int = 0, part: int = 0) -> dict:
    key_of = jax.random.split(jax.random.key(seed), 11)
    part_splits = jax.random.split(jax.random.fold_in(key_of[10], part), 11)
    return {
        "inputs": centred(part_splits[0], (TOKENS, D), 1.0, 6.0, ((0, 8), (1, 8))),
        "cotangent": centred(part_splits[1], (TOKENS, D), 1.0, 6.0, ((0, 8), (1, 8))),
        "norm_gain": jnp.clip(1.0 + 0.15 * jax.random.normal(key_of[2], (2, D), jnp.float32), 0.25, 1.75),
        "head_gain": jnp.clip(jnp.exp(jax.random.uniform(key_of[3], (2, 2, HEAD_DIM), jnp.float32, math.log(0.5), math.log(2.5))), 0.5, 2.5),
        "query_weight": centred(key_of[4], (2, D, HEADS * HEAD_DIM), D ** -0.5, 0.09375, ((2, 8),)),
        "key_weight": centred(key_of[5], (2, D, 2 * KV_HEADS * HEAD_DIM), D ** -0.5, 0.09375, ((2, 8),)),
        "output_weight": centred(key_of[6], (2, HEADS * HEAD_DIM, D), (HEADS * HEAD_DIM // 8) ** -0.5, 0.375, ((1, 8),)),
        "modality": place_ends((jax.random.randint(part_splits[7], (TOKENS,), 0, 2) < 1).astype(jnp.int32), jax.random.fold_in(part_splits[7], 1), 0, 1),
        "segments": jnp.searchsorted(jnp.cumsum(uneven(part_splits[8], SEGS, TOKENS, SEG_MOST, 2)), jnp.arange(TOKENS), side="right").astype(jnp.int32),
        "block_order": jax.random.permutation(part_splits[9], BLOCKS).astype(jnp.int32),
    }


epsilon = 1e-06

def row_norm(values, scaling):
    factor = lax.rsqrt(lax.optimization_barrier(jnp.mean(values * values, axis=-1, keepdims=True)) + epsilon)
    return (values * factor * scaling, factor)

def norm_back(values, factor, scaling, upstream):
    unit_rows = values * factor
    inner_mean = lax.optimization_barrier(jnp.mean(scaling * upstream * unit_rows, axis=-1, keepdims=True))
    return factor * (scaling * upstream - unit_rows * inner_mean)

def expert_pick(is_image, weights, operand):
    text_part = jnp.dot(operand, weights[0], preferred_element_type=jnp.float32)
    image_part = jnp.dot(operand, weights[1], preferred_element_type=jnp.float32)
    return jnp.where(is_image, image_part, text_part)

def expert_back(is_image, weights, operand):
    text_part = jnp.dot(operand, weights[0].T, preferred_element_type=jnp.float32)
    image_part = jnp.dot(operand, weights[1].T, preferred_element_type=jnp.float32)
    return jnp.where(is_image, image_part, text_part)

def reference(inputs, cotangent, norm_gain, head_gain, query_weight, key_weight, output_weight, modality, segments, block_order):
    total_rows = inputs.shape[0]
    score_scale = 1.0 / math.sqrt(HEAD_DIM)
    positions = jnp.arange(total_rows, dtype=jnp.int32)
    anchor = block_order[positions // TOK_DEV] * TOK_DEV + positions % TOK_DEV
    row_segments = segments[anchor]
    visible = row_segments[None, :] <= row_segments[:, None]
    is_image = (modality == 1)[:, None]
    head_image = is_image[:, :, None]
    rows_float = inputs.astype(jnp.float32)
    row_scaling = jnp.where(is_image, norm_gain[1][None, :], norm_gain[0][None, :])
    normed, row_factor = row_norm(rows_float, row_scaling)
    normed = normed.astype(jnp.bfloat16)
    query_raw = expert_pick(is_image, query_weight, normed).reshape(total_rows, HEADS, HEAD_DIM)
    query_scaling = jnp.where(head_image, head_gain[1, 0], head_gain[0, 0])
    query_normed, query_factor = row_norm(query_raw, query_scaling)
    query_normed = query_normed.astype(jnp.bfloat16)
    pair_raw = expert_pick(is_image, key_weight, normed).reshape(total_rows, KV_HEADS, 2, HEAD_DIM)
    key_raw = pair_raw[:, :, 0]
    value_rows = pair_raw[:, :, 1].astype(jnp.bfloat16)
    key_scaling = jnp.where(head_image, head_gain[1, 1], head_gain[0, 1])
    key_normed, key_factor = row_norm(key_raw, key_scaling)
    key_normed = key_normed.astype(jnp.bfloat16)
    head_keys = jnp.repeat(key_normed, GROUP, axis=1).transpose(1, 0, 2)
    head_values = jnp.repeat(value_rows, GROUP, axis=1).transpose(1, 0, 2)
    head_queries = query_normed.transpose(1, 0, 2)

    def weights_of(query_head, key_head):
        scores = jnp.dot(query_head, key_head.T, preferred_element_type=jnp.float32) * score_scale
        return jnp.where(visible, jnp.exp(scores), 0.0).astype(jnp.bfloat16)

    def forward_head(operands):
        query_head, key_head, value_head = operands
        weights = weights_of(query_head, key_head)
        denominator = lax.optimization_barrier(jnp.sum(weights.astype(jnp.float32), axis=1))
        numerator = jnp.dot(weights, value_head, preferred_element_type=jnp.float32)
        return ((numerator / denominator[:, None]).astype(jnp.bfloat16), denominator)
    attended, denominator = lax.map(forward_head, (head_queries, head_keys, head_values))
    attended_rows = attended.transpose(1, 0, 2).reshape(total_rows, HEADS * HEAD_DIM)
    attention_out = expert_pick(is_image, output_weight, attended_rows).astype(jnp.bfloat16)
    back_attended = expert_back(is_image, output_weight, cotangent).astype(jnp.bfloat16)
    head_backs = back_attended.reshape(total_rows, HEADS, HEAD_DIM).transpose(1, 0, 2)
    offset = lax.optimization_barrier(jnp.sum(head_backs.astype(jnp.float32) * attended.astype(jnp.float32), axis=2))

    def backward_head(operands):
        query_head, key_head, value_head, back_head, total_head, offset_head = operands
        weights = weights_of(query_head, key_head)
        probability = (weights.astype(jnp.float32) / total_head[:, None]).astype(jnp.bfloat16)
        back_prob = jnp.dot(back_head, value_head.T, preferred_element_type=jnp.float32)
        back_score = (probability.astype(jnp.float32) * (back_prob - offset_head[:, None])).astype(jnp.bfloat16)
        back_query = jnp.dot(back_score, key_head, preferred_element_type=jnp.float32) * score_scale
        back_key = jnp.dot(back_score.T, query_head, preferred_element_type=jnp.float32) * score_scale
        back_value = jnp.dot(probability.T, back_head, preferred_element_type=jnp.float32)
        return (back_query, back_key, back_value)
    back_query, back_key, back_value = lax.map(backward_head, (head_queries, head_keys, head_values, head_backs, denominator, offset))
    back_key = back_key.reshape(KV_HEADS, GROUP, total_rows, HEAD_DIM).sum(axis=1).transpose(1, 0, 2)
    back_value = back_value.reshape(KV_HEADS, GROUP, total_rows, HEAD_DIM).sum(axis=1).transpose(1, 0, 2)
    query_back = norm_back(query_raw, query_factor, query_scaling, back_query.transpose(1, 0, 2)).astype(jnp.bfloat16)
    key_back = norm_back(key_raw, key_factor, key_scaling, back_key).astype(jnp.bfloat16)
    pair_back = jnp.stack([key_back, back_value.astype(jnp.bfloat16)], axis=2).reshape(total_rows, 2 * KV_HEADS * HEAD_DIM)
    back_normed = expert_back(is_image, query_weight, query_back.reshape(total_rows, HEADS * HEAD_DIM)) + expert_back(is_image, key_weight, pair_back)
    grad_input = norm_back(rows_float, row_factor, row_scaling, back_normed).astype(jnp.bfloat16)
    return (attention_out, grad_input)
```

```python
import functools
import math

import jax
import jax.numpy as jnp
from jax import lax
from jax.experimental import pallas as pl
from jax.experimental.pallas import tpu as pltpu
from jax.sharding import PartitionSpec as P

HEAD_DIM = 128
EPSILON = 1e-06
MESH = pl.DeviceIdType.MESH
F32 = jnp.float32
BF16 = jnp.bfloat16

LEFT_A, LEFT_B, RIGHT_A, RIGHT_B, FAR_A, FAR_B, MATE_OWN, MATE_LEFT, MATE_RIGHT, MATE_FAR = range(10)
FAR, RIGHT, LEFT, OWN = range(4)


def dot(a, b):
    return jnp.dot(a, b, preferred_element_type=F32)


def dot_nt(a, b):
    return lax.dot_general(a, b, (((1,), (1,)), ((), ())), preferred_element_type=F32)


def dot_tn(a, b):
    return lax.dot_general(a, b, (((0,), (0,)), ((), ())), preferred_element_type=F32)


def remote(src, dst, send_sem, recv_sem, **device):
    return pltpu.make_async_remote_copy(
        src_ref=src,
        dst_ref=dst,
        send_sem=send_sem,
        recv_sem=recv_sem,
        device_id=device,
        device_id_type=MESH,
    )


def kernel(
    seq_size,
    tensor_size,
    order_ref,
    modality_ref,
    segments_ref,
    norm_gain_ref,
    head_gain_ref,
    inputs_ref,
    cotangent_ref,
    query_hbm,
    key_hbm,
    output_hbm,
    attention_ref,
    grad_ref,
    query_w,
    key_w,
    output_w,
    rows_buf,
    gain_buf,
    query_acc,
    key_acc,
    back_acc,
    query_raw_buf,
    key_raw_buf,
    memory_buf,
    pair_buf,
    back_buf,
    sums_stage,
    sums_mate,
    sums_hop,
    sums_out,
    sums_final,
    memory_back,
    memory_mate,
    memory_out,
    memory_in,
    partial_buf,
    inner_out,
    inner_in,
    local_sem,
    gather_send,
    gather_recv,
    memory_send,
    memory_recv,
    sums_send,
    sums_recv,
    back_send,
    back_recv,
    inner_send,
    inner_recv,
):
    seq = lax.axis_index("seq")
    me = lax.axis_index("tensor")
    core = lax.rem(me, 2)
    mate = me + 1 - 2 * core
    right = lax.rem(me + 2, tensor_size)
    left = lax.rem(me + tensor_size - 2, tensor_size)
    far = lax.rem(me + 4, tensor_size)
    mate_right = right + 1 - 2 * core
    mate_left = left + 1 - 2 * core
    mate_far = far + 1 - 2 * core
    rows, width = inputs_ref.shape
    half = rows // 2
    total_width = width * tensor_size
    scale = 1.0 / math.sqrt(HEAD_DIM)
    half_a, half_b = pl.ds(0, half), pl.ds(half, half)

    barrier = pltpu.get_barrier_semaphore()
    for step in range(1, tensor_size):
        pl.semaphore_signal(
            barrier, inc=1, device_id={"tensor": lax.rem(me + step, tensor_size)}, device_id_type=MESH
        )
    for step in range(1, seq_size):
        pl.semaphore_signal(
            barrier, inc=1, device_id={"seq": lax.rem(seq + step, seq_size)}, device_id_type=MESH
        )

    own_rows = [
        pltpu.make_async_copy(ref, rows_buf.at[k, me], local_sem.at[k])
        for k, ref in enumerate((inputs_ref, cotangent_ref))
    ]
    weights = [
        pltpu.make_async_copy(src, dst, local_sem.at[2 + k])
        for k, (src, dst) in enumerate(((query_hbm, query_w), (key_hbm, key_w), (output_hbm, output_w)))
    ]
    own_rows[0].start()
    for copy in weights:
        copy.start()
    own_rows[1].start()
    pl.semaphore_wait(barrier, tensor_size - 1 + seq_size - 1)

    def gather(k):
        own = (inputs_ref, cotangent_ref)[k]

        def to(slot, src, dst, device):
            return remote(src, dst, gather_send.at[k, slot], gather_recv.at[k, slot], tensor=device)

        def shard(slot, which, part, device):
            there = rows_buf.at[k, which] if part is None else rows_buf.at[k, which, part]
            if which is me:
                here = own if part is None else own.at[part]
            else:
                here = there
            return to(slot, here, there, device)

        return {
            LEFT_A: shard(LEFT_A, me, half_a, right),
            LEFT_B: shard(LEFT_B, me, half_b, right),
            RIGHT_A: shard(RIGHT_A, me, half_a, left),
            RIGHT_B: shard(RIGHT_B, me, half_b, left),
            FAR_A: shard(FAR_A, left, half_a, right),
            FAR_B: shard(FAR_B, right, half_b, left),
            MATE_OWN: shard(MATE_OWN, me, None, mate),
            MATE_LEFT: shard(MATE_LEFT, left, None, mate),
            MATE_RIGHT: shard(MATE_RIGHT, right, None, mate),
            MATE_FAR: shard(MATE_FAR, far, None, mate),
        }

    gathers = [gather(0), gather(1)]

    def gather_start(k):
        for slot in (LEFT_A, RIGHT_B, LEFT_B, RIGHT_A, MATE_OWN):
            gathers[k][slot].start()

    def gather_forward(k):
        copies = gathers[k]
        copies[LEFT_A].wait_recv()
        copies[FAR_A].start()
        copies[RIGHT_B].wait_recv()
        copies[FAR_B].start()

    def gather_near(k):
        copies = gathers[k]
        copies[LEFT_B].wait_recv()
        copies[MATE_LEFT].start()
        copies[RIGHT_A].wait_recv()
        copies[MATE_RIGHT].start()

    def gather_far(k):
        copies = gathers[k]
        copies[FAR_A].wait_recv()
        copies[FAR_B].wait_recv()
        copies[MATE_FAR].start()

    gather_start(0)

    row_of = lax.broadcasted_iota(jnp.int32, (rows, rows), 0)
    col_of = lax.broadcasted_iota(jnp.int32, (rows, rows), 1)
    diagonal = row_of == col_of

    def as_column(row):
        return jnp.sum(jnp.where(diagonal, row, 0.0), axis=1, keepdims=True)

    def as_row(column):
        return jnp.sum(jnp.where(diagonal, column, 0.0), axis=0, keepdims=True)

    is_image = as_column((modality_ref[...] == 1).astype(F32)) > 0.5
    image_pick = jnp.broadcast_to(is_image, (rows, HEAD_DIM))
    for k in range(tensor_size):
        gain_buf[k, 0:2, :] = norm_gain_ref[:, k * width : (k + 1) * width]

    def segments_of(block):
        return segments_ref[pl.ds(order_ref[block], 1), :].astype(F32)

    key_segments = jnp.concatenate([segments_of(k) for k in range(seq_size)], axis=1)
    query_segments = as_column(segments_of(seq))

    def gain_of(slot):
        return jnp.where(is_image, gain_buf[slot, 1:2, :], gain_buf[slot, 0:1, :])

    query_acc[...] = jnp.zeros_like(query_acc)
    key_acc[...] = jnp.zeros_like(key_acc)
    back_acc[...] = jnp.zeros_like(back_acc)

    def project(slot, squares):
        x = rows_buf[0, slot].astype(F32)
        scaled = (x * gain_of(slot)).astype(BF16)
        span = pl.ds(pl.multiple_of(slot * width, 64), width)
        for e in range(2):
            query_acc[e] += dot(scaled, query_w[e, span, :])
            key_acc[e] += dot(scaled, key_w[e, span, :])
        return squares + jnp.sum(x * x, axis=1, keepdims=True)

    squares = jnp.zeros((rows, 1), F32)
    own_rows[0].wait()
    weights[0].wait()
    weights[1].wait()
    squares = project(me, squares)
    gather_forward(0)
    gathers[0][MATE_OWN].wait_recv()
    squares = project(mate, squares)
    gather_near(0)
    squares = project(left, squares)
    squares = project(right, squares)
    gathers[0][MATE_LEFT].wait_recv()
    squares = project(mate_left, squares)
    gathers[0][MATE_RIGHT].wait_recv()
    squares = project(mate_right, squares)
    gather_far(0)
    gather_start(1)
    squares = project(far, squares)
    gathers[0][MATE_FAR].wait_recv()
    squares = project(mate_far, squares)

    row_factor = lax.rsqrt(squares / total_width + EPSILON)

    def picked(acc, columns):
        return jnp.where(image_pick, acc[1, :, columns], acc[0, :, columns]) * row_factor

    def head_factor(raw):
        return lax.rsqrt(jnp.mean(raw * raw, axis=-1, keepdims=True) + EPSILON)

    def head_gain(kind):
        return jnp.where(image_pick, head_gain_ref[1, kind : kind + 1, :], head_gain_ref[0, kind : kind + 1, :])

    key_raw = picked(key_acc, slice(None))
    key_raw_buf[...] = key_raw
    key_normed = key_raw * head_factor(key_raw) * head_gain(1)
    memory_buf[core, seq] = jnp.where(core == 0, key_normed, key_raw).astype(BF16)

    seq_steps = range(1, seq_size)
    memory_sends = {
        step: remote(
            memory_buf.at[core, seq],
            memory_buf.at[core, seq],
            memory_send.at[0, step],
            memory_recv.at[0, step],
            seq=lax.rem(seq + step, seq_size),
        )
        for step in seq_steps
    }
    memory_mates = {}
    for step in range(seq_size):
        block = lax.rem(seq + seq_size - step, seq_size)
        memory_mates[step] = remote(
            memory_buf.at[core, block],
            memory_buf.at[core, block],
            memory_send.at[1, step],
            memory_recv.at[1, step],
            tensor=mate,
        )
    for step in seq_steps:
        memory_sends[step].start()
    memory_mates[0].start()

    heads = query_acc.shape[2] // HEAD_DIM
    for h in range(heads):
        raw = picked(query_acc, slice(h * HEAD_DIM, (h + 1) * HEAD_DIM))
        query_raw_buf[h * rows : (h + 1) * rows] = raw
    query_gain = jnp.concatenate([head_gain(0)] * heads, axis=0)
    query_raw = query_raw_buf[...]
    query_normed = (query_raw * head_factor(query_raw) * query_gain).astype(BF16)

    def back_project(first, second):
        pair_buf[:, 0:width] = rows_buf[1, first].astype(F32)
        pair_buf[:, width : 2 * width] = rows_buf[1, second].astype(F32)
        both = pair_buf[...].astype(BF16)
        span = pl.ds(pl.multiple_of(first * width, 128), 2 * width)
        for e in range(2):
            back_acc[e] += dot_nt(both, output_w[e, :, span])

    gather_forward(1)
    gather_near(1)
    own_rows[1].wait()
    weights[2].wait()
    gathers[1][MATE_OWN].wait_recv()
    back_project(me - core, me - core + 1)

    for step in seq_steps:
        memory_sends[step].wait_recv()
        memory_mates[step].start()
    for step in range(seq_size):
        memory_mates[step].wait_recv()

    all_rows = seq_size * rows
    keys = memory_buf[0].reshape(all_rows, HEAD_DIM)
    values = memory_buf[1].reshape(all_rows, HEAD_DIM)
    visible = key_segments <= jnp.concatenate([query_segments] * heads, axis=0)
    scores = dot_nt(query_normed, keys) * scale
    attention_weights = jnp.where(visible, jnp.exp(scores), 0.0).astype(BF16)
    denominator = jnp.sum(attention_weights.astype(F32), axis=1, keepdims=True)
    attended = (dot(attention_weights, values) / denominator).astype(BF16)

    places = {FAR: far, RIGHT: right, LEFT: left, OWN: me}

    def by_expert(parts, picks):
        zero = jnp.zeros_like(parts)
        return jnp.concatenate(
            [jnp.where(picks, zero, parts), jnp.where(picks, parts, zero)], axis=1
        ).astype(BF16)

    def sums_copies(k):
        def to(slot, src, dst, device):
            return remote(src, dst, sums_send.at[k, slot], sums_recv.at[k, slot], tensor=device)

        copies = {("mate", p): to(p, sums_stage.at[k, p, 1 - core], sums_mate.at[k, p], mate) for p in range(4)}
        copies["far_a"] = to(4, sums_out.at[k, FAR, half_a], sums_hop.at[k, 0], right)
        copies["far_b"] = to(5, sums_out.at[k, FAR, half_b], sums_hop.at[k, 1], left)
        copies["right_a"] = to(6, sums_out.at[k, RIGHT, half_a], sums_final.at[k, 0, half_a], right)
        copies["right_b"] = to(7, sums_out.at[k, RIGHT, half_b], sums_final.at[k, 0, half_b], right)
        copies["left_a"] = to(8, sums_out.at[k, LEFT, half_a], sums_final.at[k, 1, half_a], left)
        copies["left_b"] = to(9, sums_out.at[k, LEFT, half_b], sums_final.at[k, 1, half_b], left)
        return copies

    sums = [sums_copies(0), sums_copies(1)]

    def chip_sum(k, place):
        return sums_stage[k, place, core].astype(F32) + sums_mate[k, place].astype(F32)

    def sums_first(k):
        copies = sums[k]
        copies["mate", FAR].wait_recv()
        sums_out[k, FAR] = chip_sum(k, FAR).astype(BF16)
        copies["far_a"].start()
        copies["far_b"].start()

    def sums_second(k):
        copies = sums[k]
        for place, name in ((RIGHT, "right_b"), (LEFT, "left_a")):
            copies["mate", place].wait_recv()
            sums_out[k, place] = chip_sum(k, place).astype(BF16)
            copies[name].start()

    def sums_third(k):
        copies = sums[k]
        for place, hop, name, rows_of in ((RIGHT, 0, "far_a", half_a), (LEFT, 1, "far_b", half_b)):
            copies[name].wait_recv()
            first = sums_stage[k, place, core, rows_of].astype(F32) + sums_mate[k, place, rows_of].astype(F32)
            sums_out[k, place, rows_of] = (first + sums_hop[k, hop].astype(F32)).astype(BF16)
            copies["right_a" if place == RIGHT else "left_b"].start()

    def sums_last(k):
        copies = sums[k]
        copies["mate", OWN].wait_recv()
        for name in ("right_b", "left_a", "right_a", "left_b"):
            copies[name].wait_recv()
        return chip_sum(k, OWN) + sums_final[k, 0].astype(F32) + sums_final[k, 1].astype(F32)

    head_rows = [slice(h * rows, (h + 1) * rows) for h in range(heads)]

    def side_by_side(stacked):
        return jnp.concatenate([stacked[r] for r in head_rows], axis=1)

    wide_pick = jnp.broadcast_to(is_image, (rows, heads * HEAD_DIM))
    attended_parts = by_expert(side_by_side(attended.astype(F32)), wide_pick)
    depth = heads * HEAD_DIM
    for place in (FAR, RIGHT, LEFT, OWN):
        span = pl.ds(pl.multiple_of((places[place] - core) * width, 128), 2 * width)
        block = dot(attended_parts[:, :depth], output_w[0, :, span]) + dot(
            attended_parts[:, depth:], output_w[1, :, span]
        )
        sums_stage[0, place, 0] = block[:, :width].astype(BF16)
        sums_stage[0, place, 1] = pltpu.roll(block, width, 1)[:, :width].astype(BF16)
        sums[0]["mate", place].start()

    gathers[1][MATE_LEFT].wait_recv()
    back_project(left - core, left - core + 1)
    gathers[1][MATE_RIGHT].wait_recv()
    back_project(right - core, right - core + 1)
    sums_first(0)
    gather_far(1)
    gathers[1][MATE_FAR].wait_recv()
    back_project(far - core, far - core + 1)
    sums_second(0)

    for h in range(heads):
        columns = slice(h * HEAD_DIM, (h + 1) * HEAD_DIM)
        back_buf[head_rows[h]] = jnp.where(image_pick, back_acc[1, :, columns], back_acc[0, :, columns]).astype(BF16)
    back_attended = back_buf[...]
    offset = jnp.sum(back_attended.astype(F32) * attended.astype(F32), axis=1, keepdims=True)
    probability = (attention_weights.astype(F32) / denominator).astype(BF16)
    back_probability = dot_nt(back_attended, values)
    back_score = (probability.astype(F32) * (back_probability - offset)).astype(BF16)
    memory_back[0] = (dot_tn(back_score, query_normed) * scale).astype(BF16).reshape(seq_size, rows, HEAD_DIM)
    memory_back[1] = dot_tn(probability, back_attended).astype(BF16).reshape(seq_size, rows, HEAD_DIM)
    back_to_mate = remote(
        memory_back.at[1 - core], memory_mate, back_send.at[0], back_recv.at[0], tensor=mate
    )
    back_to_mate.start()

    back_query = dot(back_score, keys) * scale
    query_factor = head_factor(query_raw)
    query_unit = query_raw * query_factor
    weighted = query_gain * back_query
    query_back = query_factor * (
        weighted - query_unit * jnp.mean(weighted * query_unit, axis=-1, keepdims=True)
    )
    query_parts = by_expert(side_by_side(query_back), wide_pick)

    back_to_mate.wait_recv()
    own_sum = memory_back[core].astype(F32) + memory_mate[...].astype(F32)
    memory_out[...] = own_sum.astype(BF16)
    back_sends = {}
    for step in seq_steps:
        block = lax.rem(seq + step, seq_size)
        back_sends[step] = remote(
            memory_out.at[block], memory_in.at[step], back_send.at[step], back_recv.at[step], seq=block
        )
        back_sends[step].start()

    sums_third(0)

    def slots_of(place):
        first = places[place] - core
        return first, first + 1

    for place in (FAR, RIGHT, LEFT, OWN):
        for parity, slot in enumerate(slots_of(place)):
            span = pl.ds(pl.multiple_of(slot * width, 64), width)
            partial_buf[place, parity] = dot_nt(query_parts[:, :depth], query_w[0, span, :]) + dot_nt(
                query_parts[:, depth:], query_w[1, span, :]
            )

    attention_ref[...] = sums_last(0).astype(BF16)

    slice_grad = memory_out[seq].astype(F32)
    for step in seq_steps:
        back_sends[step].wait_recv()
        slice_grad = slice_grad + memory_in[step].astype(F32)
    key_raw = key_raw_buf[...]
    key_factor = head_factor(key_raw)
    key_unit = key_raw * key_factor
    weighted = head_gain(1) * slice_grad
    key_back = key_factor * (weighted - key_unit * jnp.mean(weighted * key_unit, axis=-1, keepdims=True))
    slice_back = jnp.where(core == 0, key_back, slice_grad)
    slice_parts = by_expert(slice_back, image_pick)

    inner = jnp.zeros((rows, 1), F32)
    for place in (FAR, RIGHT, LEFT, OWN):
        for parity, slot in enumerate(slots_of(place)):
            span = pl.ds(pl.multiple_of(slot * width, 64), width)
            part = (
                partial_buf[place, parity]
                + dot_nt(slice_parts[:, :HEAD_DIM], key_w[0, span, :])
                + dot_nt(slice_parts[:, HEAD_DIM:], key_w[1, span, :])
            )
            sums_stage[1, place, parity] = part.astype(BF16)
            partial_buf[place, parity] = part
        sums[1]["mate", place].start()
    sums_first(1)
    sums_second(1)
    for place in (FAR, RIGHT, LEFT, OWN):
        for parity, slot in enumerate(slots_of(place)):
            scaled = rows_buf[0, slot].astype(F32) * gain_of(slot)
            inner = inner + jnp.sum(scaled * partial_buf[place, parity], axis=1, keepdims=True)
    inner_row = as_row(inner)
    inner_out[...] = jnp.broadcast_to(inner_row, inner_out.shape)
    inner_sends = {}
    for step in range(1, tensor_size):
        inner_sends[step] = remote(
            inner_out,
            inner_in.at[step],
            inner_send.at[step],
            inner_recv.at[step],
            tensor=lax.rem(me + step, tensor_size),
        )
        inner_sends[step].start()
    sums_third(1)
    for step in range(1, tensor_size):
        inner_sends[step].wait_recv()
        inner_row = inner_row + inner_in[step, 0:1, :]
    inner_mean = row_factor * as_column(inner_row) / total_width
    local_gain = gain_of(me)
    unit_rows = rows_buf[0, me].astype(F32) * row_factor
    shift = unit_rows * inner_mean
    grad_ref[...] = (row_factor * (local_gain * sums_last(1) - shift)).astype(BF16)

    for copies in (*gathers, *sums, memory_sends, memory_mates, back_sends, inner_sends):
        for copy in copies.values():
            copy.wait_send()
    back_to_mate.wait_send()


def solution(mesh):
    seq_size, tensor_size = mesh.shape["seq"], mesh.shape["tensor"]

    def local(
        inputs,
        cotangent,
        norm_gain,
        head_gain,
        query_weight,
        key_weight,
        output_weight,
        modality,
        segments,
        block_order,
    ):
        rows, width = inputs.shape
        heads = query_weight.shape[2] // HEAD_DIM
        vmem = pl.BlockSpec(memory_space=pltpu.VMEM)
        anywhere = pl.BlockSpec(memory_space=pl.ANY)
        dma = pltpu.SemaphoreType.DMA
        shape = jax.ShapeDtypeStruct((rows, width), BF16)
        block = (seq_size, rows, HEAD_DIM)
        return pl.pallas_call(
            functools.partial(kernel, seq_size, tensor_size),
            out_shape=(shape, shape),
            in_specs=[pl.BlockSpec(memory_space=pltpu.SMEM)] + [vmem] * 4 + [anywhere] * 5,
            out_specs=(vmem, vmem),
            scratch_shapes=[
                pltpu.VMEM(query_weight.shape, BF16),
                pltpu.VMEM(key_weight.shape, BF16),
                pltpu.VMEM(output_weight.shape, BF16),
                pltpu.VMEM((2, tensor_size, rows, width), BF16),
                pltpu.VMEM((tensor_size, 8, width), F32),
                pltpu.VMEM((2, rows, heads * HEAD_DIM), F32),
                pltpu.VMEM((2, rows, HEAD_DIM), F32),
                pltpu.VMEM((2, rows, heads * HEAD_DIM), F32),
                pltpu.VMEM((heads * rows, HEAD_DIM), F32),
                pltpu.VMEM((rows, HEAD_DIM), F32),
                pltpu.VMEM((2, *block), BF16),
                pltpu.VMEM((rows, 2 * width), F32),
                pltpu.VMEM((heads * rows, HEAD_DIM), BF16),
                pltpu.VMEM((2, 4, 2, rows, width), BF16),
                pltpu.VMEM((2, 4, rows, width), BF16),
                pltpu.VMEM((2, 2, rows // 2, width), BF16),
                pltpu.VMEM((2, 3, rows, width), BF16),
                pltpu.VMEM((2, 2, rows, width), BF16),
                pltpu.VMEM((2, *block), BF16),
                pltpu.VMEM(block, BF16),
                pltpu.VMEM(block, BF16),
                pltpu.VMEM(block, BF16),
                pltpu.VMEM((4, 2, rows, width), F32),
                pltpu.VMEM((8, rows), F32),
                pltpu.VMEM((tensor_size, 8, rows), F32),
                dma((5,)),
                dma((2, 10)),
                dma((2, 10)),
                dma((2, seq_size)),
                dma((2, seq_size)),
                dma((2, 10)),
                dma((2, 10)),
                dma((seq_size,)),
                dma((seq_size,)),
                dma((tensor_size,)),
                dma((tensor_size,)),
            ],
            compiler_params=pltpu.CompilerParams(collective_id=0, has_side_effects=True),
        )(
            block_order,
            modality.reshape(1, rows),
            segments.reshape(seq_size, rows),
            norm_gain,
            head_gain,
            inputs,
            cotangent,
            query_weight,
            key_weight,
            output_weight,
        )

    return jax.shard_map(
        local,
        mesh=mesh,
        in_specs=(
            P(("dp", "seq"), "tensor"),
            P(("dp", "seq"), "tensor"),
            P(),
            P(),
            P(None, None, "tensor"),
            P(None, None, "tensor"),
            P(None, "tensor", None),
            P(("dp", "seq")),
            P("dp"),
            P("dp"),
        ),
        out_specs=(P(("dp", "seq"), "tensor"), P(("dp", "seq"), "tensor")),
        check_vma=False,
    )
```

```python
import functools
import math

import jax
import jax.numpy as jnp
from jax import lax
from jax.experimental import pallas as pl
from jax.experimental.pallas import tpu as pltpu
from jax.sharding import PartitionSpec as P

HEAD_DIM = 128
EPSILON = 1e-06
MESH = pl.DeviceIdType.MESH
F32 = jnp.float32
BF16 = jnp.bfloat16

LEFT_A, LEFT_B, RIGHT_A, RIGHT_B, FAR_A, FAR_B, MATE_OWN, MATE_LEFT, MATE_RIGHT, MATE_FAR = range(10)
FAR, RIGHT, LEFT, OWN = range(4)


def dot(a, b):
    return jnp.dot(a, b, preferred_element_type=F32)


def dot_nt(a, b):
    return lax.dot_general(a, b, (((1,), (1,)), ((), ())), preferred_element_type=F32)


def dot_tn(a, b):
    return lax.dot_general(a, b, (((0,), (0,)), ((), ())), preferred_element_type=F32)


def remote(src, dst, send_sem, recv_sem, **device):
    return pltpu.make_async_remote_copy(
        src_ref=src,
        dst_ref=dst,
        send_sem=send_sem,
        recv_sem=recv_sem,
        device_id=device,
        device_id_type=MESH,
    )


def kernel(
    seq_size,
    tensor_size,
    order_ref,
    modality_ref,
    segments_ref,
    norm_gain_ref,
    head_gain_ref,
    inputs_ref,
    cotangent_ref,
    query_hbm,
    key_hbm,
    output_hbm,
    attention_ref,
    grad_ref,
    query_w,
    key_w,
    output_w,
    rows_buf,
    gain_buf,
    query_acc,
    key_acc,
    back_acc,
    query_raw_buf,
    key_raw_buf,
    memory_buf,
    back_buf,
    sums_stage,
    sums_mate,
    sums_hop,
    sums_out,
    sums_final,
    memory_back,
    memory_mate,
    memory_out,
    memory_in,
    partial_buf,
    inner_out,
    inner_in,
    local_sem,
    gather_send,
    gather_recv,
    memory_send,
    memory_recv,
    sums_send,
    sums_recv,
    back_send,
    back_recv,
    inner_send,
    inner_recv,
):
    seq = lax.axis_index("seq")
    me = lax.axis_index("tensor")
    core = lax.rem(me, 2)
    mate = me + 1 - 2 * core
    right = lax.rem(me + 2, tensor_size)
    left = lax.rem(me + tensor_size - 2, tensor_size)
    far = lax.rem(me + 4, tensor_size)
    mate_right = right + 1 - 2 * core
    mate_left = left + 1 - 2 * core
    mate_far = far + 1 - 2 * core
    width, rows = inputs_ref.shape
    half = width // 2
    total_width = width * tensor_size
    scale = 1.0 / math.sqrt(HEAD_DIM)
    half_a, half_b = pl.ds(0, half), pl.ds(half, half)

    def shard_of(slot, part=0, size=width):
        return pl.ds(pl.multiple_of(slot * width + part * half, 32), size)

    barrier = pltpu.get_barrier_semaphore()
    for step in range(1, tensor_size):
        pl.semaphore_signal(
            barrier, inc=1, device_id={"tensor": lax.rem(me + step, tensor_size)}, device_id_type=MESH
        )
    for step in range(1, seq_size):
        pl.semaphore_signal(
            barrier, inc=1, device_id={"seq": lax.rem(seq + step, seq_size)}, device_id_type=MESH
        )

    own_rows = [
        pltpu.make_async_copy(ref, rows_buf.at[k, shard_of(me)], local_sem.at[k])
        for k, ref in enumerate((inputs_ref, cotangent_ref))
    ]
    weights = [
        pltpu.make_async_copy(src, dst, local_sem.at[2 + k])
        for k, (src, dst) in enumerate(((query_hbm, query_w), (key_hbm, key_w), (output_hbm, output_w)))
    ]
    own_rows[0].start()
    for copy in weights:
        copy.start()
    own_rows[1].start()
    pl.semaphore_wait(barrier, tensor_size - 1 + seq_size - 1)

    def gather(k):
        own = (inputs_ref, cotangent_ref)[k]

        def to(slot, src, dst, device):
            return remote(src, dst, gather_send.at[k, slot], gather_recv.at[k, slot], tensor=device)

        def shard(slot, which, part, device):
            if part is None:
                there, here = rows_buf.at[k, shard_of(which)], own
            else:
                there = rows_buf.at[k, shard_of(which, part, half)]
                here = own.at[pl.ds(part * half, half)]
            if which is not me:
                here = there
            return to(slot, here, there, device)

        return {
            LEFT_A: shard(LEFT_A, me, 0, right),
            LEFT_B: shard(LEFT_B, me, 1, right),
            RIGHT_A: shard(RIGHT_A, me, 0, left),
            RIGHT_B: shard(RIGHT_B, me, 1, left),
            FAR_A: shard(FAR_A, left, 0, right),
            FAR_B: shard(FAR_B, right, 1, left),
            MATE_OWN: shard(MATE_OWN, me, None, mate),
            MATE_LEFT: shard(MATE_LEFT, left, None, mate),
            MATE_RIGHT: shard(MATE_RIGHT, right, None, mate),
            MATE_FAR: shard(MATE_FAR, far, None, mate),
        }

    gathers = [gather(0), gather(1)]

    def gather_start(k):
        for slot in (LEFT_A, RIGHT_B, LEFT_B, RIGHT_A, MATE_OWN):
            gathers[k][slot].start()

    def gather_forward(k):
        copies = gathers[k]
        copies[LEFT_A].wait_recv()
        copies[FAR_A].start()
        copies[RIGHT_B].wait_recv()
        copies[FAR_B].start()

    def gather_near(k):
        copies = gathers[k]
        copies[LEFT_B].wait_recv()
        copies[MATE_LEFT].start()
        copies[RIGHT_A].wait_recv()
        copies[MATE_RIGHT].start()

    def gather_far(k):
        copies = gathers[k]
        copies[FAR_A].wait_recv()
        copies[FAR_B].wait_recv()
        copies[MATE_FAR].start()

    gather_start(0)

    row_of = lax.broadcasted_iota(jnp.int32, (rows, rows), 0)
    col_of = lax.broadcasted_iota(jnp.int32, (rows, rows), 1)
    diagonal = row_of == col_of

    def as_column(row):
        return jnp.sum(jnp.where(diagonal, row, 0.0), axis=1, keepdims=True)

    image_row = (modality_ref[...] == 1).astype(F32)
    is_image = as_column(image_row) > 0.5
    image_pick = jnp.broadcast_to(is_image, (rows, HEAD_DIM))
    image_pick_t = jnp.broadcast_to(image_row > 0.5, (HEAD_DIM, rows))
    for k in range(total_width // HEAD_DIM):
        columns = slice(k * HEAD_DIM, (k + 1) * HEAD_DIM)
        gain_buf[columns, :] = jnp.where(image_pick, norm_gain_ref[1:2, columns], norm_gain_ref[0:1, columns]).T

    def segments_of(block):
        return segments_ref[pl.ds(order_ref[block], 1), :].astype(F32)

    key_segments = jnp.concatenate([segments_of(k) for k in range(seq_size)], axis=1)
    query_segments = as_column(segments_of(seq))

    query_acc[...] = jnp.zeros_like(query_acc)
    key_acc[...] = jnp.zeros_like(key_acc)
    back_acc[...] = jnp.zeros_like(back_acc)

    def chip_of(slot):
        return pl.ds(pl.multiple_of((slot - core) * width, 2 * width), 2 * width)

    def project(slot, squares):
        span = chip_of(slot)
        x = rows_buf[0, span, :].astype(F32)
        scaled = (x * gain_buf[span, :]).T.astype(BF16)
        for e in range(2):
            query_acc[e] += dot(scaled, query_w[e, span, :])
            key_acc[e] += dot(scaled, key_w[e, span, :])
        return squares + jnp.sum(x * x, axis=0, keepdims=True)

    squares = jnp.zeros((1, rows), F32)
    with jax.named_scope("gather_own"):
        own_rows[0].wait()
        weights[0].wait()
        weights[1].wait()
        gather_forward(0)
        gathers[0][MATE_OWN].wait_recv()
    with jax.named_scope("project_own"):
        squares = project(me, squares)
    with jax.named_scope("gather_near"):
        gather_near(0)
        gathers[0][MATE_LEFT].wait_recv()
    with jax.named_scope("project_left"):
        squares = project(left, squares)
    with jax.named_scope("gather_right"):
        gathers[0][MATE_RIGHT].wait_recv()
    with jax.named_scope("project_right"):
        squares = project(right, squares)
    with jax.named_scope("gather_far"):
        gather_far(0)
    with jax.named_scope("gather_far_mate"):
        gather_start(1)
        gathers[0][MATE_FAR].wait_recv()
    with jax.named_scope("project_far"):
        squares = project(far, squares)

    factor_row = lax.rsqrt(squares / total_width + EPSILON)
    row_factor = as_column(factor_row)

    def picked(acc, columns):
        return jnp.where(image_pick, acc[1, :, columns], acc[0, :, columns]) * row_factor

    def head_factor(raw):
        return lax.rsqrt(jnp.mean(raw * raw, axis=-1, keepdims=True) + EPSILON)

    def head_gain(kind):
        return jnp.where(image_pick, head_gain_ref[1, kind : kind + 1, :], head_gain_ref[0, kind : kind + 1, :])

    key_raw = picked(key_acc, slice(None))
    key_raw_buf[...] = key_raw
    key_normed = key_raw * head_factor(key_raw) * head_gain(1)
    memory_buf[core, seq] = jnp.where(core == 0, key_normed, key_raw).astype(BF16)

    seq_steps = range(1, seq_size)
    memory_sends = {
        step: remote(
            memory_buf.at[core, seq],
            memory_buf.at[core, seq],
            memory_send.at[0, step],
            memory_recv.at[0, step],
            seq=lax.rem(seq + step, seq_size),
        )
        for step in seq_steps
    }
    memory_mates = {}
    for step in range(seq_size):
        block = lax.rem(seq + seq_size - step, seq_size)
        memory_mates[step] = remote(
            memory_buf.at[core, block],
            memory_buf.at[core, block],
            memory_send.at[1, step],
            memory_recv.at[1, step],
            tensor=mate,
        )
    for step in seq_steps:
        memory_sends[step].start()
    memory_mates[0].start()

    heads = query_acc.shape[2] // HEAD_DIM
    for h in range(heads):
        raw = picked(query_acc, slice(h * HEAD_DIM, (h + 1) * HEAD_DIM))
        query_raw_buf[h * rows : (h + 1) * rows] = raw
    query_gain = jnp.concatenate([head_gain(0)] * heads, axis=0)
    query_raw = query_raw_buf[...]
    query_normed = (query_raw * head_factor(query_raw) * query_gain).astype(BF16)

    def back_project(slot):
        span = chip_of(slot)
        for e in range(2):
            back_acc[e] += dot(output_w[e, :, span], rows_buf[1, span, :])

    gather_forward(1)
    gather_near(1)
    own_rows[1].wait()
    weights[2].wait()
    gathers[1][MATE_OWN].wait_recv()
    back_project(me)

    for step in seq_steps:
        memory_sends[step].wait_recv()
        memory_mates[step].start()
    for step in range(seq_size):
        memory_mates[step].wait_recv()

    all_rows = seq_size * rows
    keys = memory_buf[0].reshape(all_rows, HEAD_DIM)
    values = memory_buf[1].reshape(all_rows, HEAD_DIM)
    visible = key_segments <= jnp.concatenate([query_segments] * heads, axis=0)
    scores = dot_nt(query_normed, keys) * scale
    attention_weights = jnp.where(visible, jnp.exp(scores), 0.0).astype(BF16)
    denominator = jnp.sum(attention_weights.astype(F32), axis=1, keepdims=True)
    attended = (dot(attention_weights, values) / denominator).astype(BF16)

    places = {FAR: far, RIGHT: right, LEFT: left, OWN: me}

    def by_expert(parts, picks, axis):
        zero = jnp.zeros_like(parts)
        return jnp.concatenate(
            [jnp.where(picks, zero, parts), jnp.where(picks, parts, zero)], axis=axis
        ).astype(BF16)

    def sums_copies(k):
        def to(slot, src, dst, device):
            return remote(src, dst, sums_send.at[k, slot], sums_recv.at[k, slot], tensor=device)

        copies = {("mate", p): to(p, sums_stage.at[k, p, 1 - core], sums_mate.at[k, p], mate) for p in range(4)}
        copies["far_a"] = to(4, sums_out.at[k, FAR, half_a], sums_hop.at[k, 0], right)
        copies["far_b"] = to(5, sums_out.at[k, FAR, half_b], sums_hop.at[k, 1], left)
        copies["right_a"] = to(6, sums_out.at[k, RIGHT, half_a], sums_final.at[k, 0, half_a], right)
        copies["right_b"] = to(7, sums_out.at[k, RIGHT, half_b], sums_final.at[k, 0, half_b], right)
        copies["left_a"] = to(8, sums_out.at[k, LEFT, half_a], sums_final.at[k, 1, half_a], left)
        copies["left_b"] = to(9, sums_out.at[k, LEFT, half_b], sums_final.at[k, 1, half_b], left)
        return copies

    sums = [sums_copies(0), sums_copies(1)]

    def chip_sum(k, place):
        return sums_stage[k, place, core].astype(F32) + sums_mate[k, place].astype(F32)

    def sums_first(k):
        copies = sums[k]
        copies["mate", FAR].wait_recv()
        sums_out[k, FAR] = chip_sum(k, FAR).astype(BF16)
        copies["far_a"].start()
        copies["far_b"].start()

    def sums_second(k):
        copies = sums[k]
        for place, name in ((RIGHT, "right_b"), (LEFT, "left_a")):
            copies["mate", place].wait_recv()
            sums_out[k, place] = chip_sum(k, place).astype(BF16)
            copies[name].start()

    def sums_third(k):
        copies = sums[k]
        for place, hop, name, rows_of in ((RIGHT, 0, "far_a", half_a), (LEFT, 1, "far_b", half_b)):
            copies[name].wait_recv()
            first = sums_stage[k, place, core, rows_of].astype(F32) + sums_mate[k, place, rows_of].astype(F32)
            sums_out[k, place, rows_of] = (first + sums_hop[k, hop].astype(F32)).astype(BF16)
            copies["right_a" if place == RIGHT else "left_b"].start()

    def sums_last(k):
        copies = sums[k]
        copies["mate", OWN].wait_recv()
        for name in ("right_b", "left_a", "right_a", "left_b"):
            copies[name].wait_recv()
        return chip_sum(k, OWN) + sums_final[k, 0].astype(F32) + sums_final[k, 1].astype(F32)

    head_rows = [slice(h * rows, (h + 1) * rows) for h in range(heads)]

    def side_by_side(stacked):
        return jnp.concatenate([stacked[r] for r in head_rows], axis=1)

    wide_pick = jnp.broadcast_to(is_image, (rows, heads * HEAD_DIM))
    attended_parts = by_expert(side_by_side(attended.astype(F32)), wide_pick, 1)
    depth = heads * HEAD_DIM
    for place in (FAR, RIGHT, LEFT, OWN):
        span = chip_of(places[place])
        block = dot(attended_parts[:, :depth], output_w[0, :, span]) + dot(
            attended_parts[:, depth:], output_w[1, :, span]
        )
        sums_stage[0, place] = block.T.astype(BF16).reshape(2, width, rows)
        sums[0]["mate", place].start()

    gathers[1][MATE_LEFT].wait_recv()
    back_project(left)
    gathers[1][MATE_RIGHT].wait_recv()
    back_project(right)
    sums_first(0)
    gather_far(1)
    gathers[1][MATE_FAR].wait_recv()
    back_project(far)
    sums_second(0)

    for h in range(heads):
        columns = slice(h * HEAD_DIM, (h + 1) * HEAD_DIM)
        back_buf[head_rows[h]] = jnp.where(image_pick_t, back_acc[1, columns, :], back_acc[0, columns, :]).T.astype(BF16)
    back_attended = back_buf[...]
    offset = jnp.sum(back_attended.astype(F32) * attended.astype(F32), axis=1, keepdims=True)
    probability = (attention_weights.astype(F32) / denominator).astype(BF16)
    back_probability = dot_nt(back_attended, values)
    back_score = (probability.astype(F32) * (back_probability - offset)).astype(BF16)
    memory_back[0] = (dot_tn(back_score, query_normed) * scale).astype(BF16).reshape(seq_size, rows, HEAD_DIM)
    memory_back[1] = dot_tn(probability, back_attended).astype(BF16).reshape(seq_size, rows, HEAD_DIM)
    back_to_mate = remote(
        memory_back.at[1 - core], memory_mate, back_send.at[0], back_recv.at[0], tensor=mate
    )
    back_to_mate.start()

    back_query = dot(back_score, keys) * scale
    query_factor = head_factor(query_raw)
    query_unit = query_raw * query_factor
    weighted = query_gain * back_query
    query_back = query_factor * (
        weighted - query_unit * jnp.mean(weighted * query_unit, axis=-1, keepdims=True)
    )
    back_columns = jnp.concatenate([query_back[r].T for r in head_rows], axis=0)
    query_parts = by_expert(back_columns, jnp.concatenate([image_pick_t] * heads, axis=0), 0)

    back_to_mate.wait_recv()
    own_sum = memory_back[core].astype(F32) + memory_mate[...].astype(F32)
    memory_out[...] = own_sum.astype(BF16)
    back_sends = {}
    for step in seq_steps:
        block = lax.rem(seq + step, seq_size)
        back_sends[step] = remote(
            memory_out.at[block], memory_in.at[step], back_send.at[step], back_recv.at[step], seq=block
        )
        back_sends[step].start()

    sums_third(0)

    for place in (FAR, RIGHT, LEFT, OWN):
        span = chip_of(places[place])
        part = dot(query_w[0, span, :], query_parts[:depth]) + dot(query_w[1, span, :], query_parts[depth:])
        partial_buf[place] = part

    attention_ref[...] = sums_last(0).astype(BF16)

    slice_grad = memory_out[seq].astype(F32)
    for step in seq_steps:
        back_sends[step].wait_recv()
        slice_grad = slice_grad + memory_in[step].astype(F32)
    key_raw = key_raw_buf[...]
    key_factor = head_factor(key_raw)
    key_unit = key_raw * key_factor
    weighted = head_gain(1) * slice_grad
    key_back = key_factor * (weighted - key_unit * jnp.mean(weighted * key_unit, axis=-1, keepdims=True))
    slice_back = jnp.where(core == 0, key_back, slice_grad)
    slice_parts = by_expert(slice_back.T, image_pick_t, 0)

    for place in (FAR, RIGHT, LEFT, OWN):
        span = chip_of(places[place])
        part = (
            partial_buf[place]
            + dot(key_w[0, span, :], slice_parts[:HEAD_DIM])
            + dot(key_w[1, span, :], slice_parts[HEAD_DIM:])
        )
        sums_stage[1, place] = part.astype(BF16).reshape(2, width, rows)
        partial_buf[place] = part
        sums[1]["mate", place].start()
    sums_first(1)
    sums_second(1)
    inner_row = jnp.zeros((1, rows), F32)
    for place in (FAR, RIGHT, LEFT, OWN):
        span = chip_of(places[place])
        scaled = rows_buf[0, span, :].astype(F32) * gain_buf[span, :]
        inner_row = inner_row + jnp.sum(scaled * partial_buf[place], axis=0, keepdims=True)
    inner_out[...] = jnp.broadcast_to(inner_row, inner_out.shape)
    inner_sends = {}
    for step in range(1, tensor_size):
        inner_sends[step] = remote(
            inner_out,
            inner_in.at[step],
            inner_send.at[step],
            inner_recv.at[step],
            tensor=lax.rem(me + step, tensor_size),
        )
        inner_sends[step].start()
    sums_third(1)
    for step in range(1, tensor_size):
        inner_sends[step].wait_recv()
        inner_row = inner_row + inner_in[step, 0:1, :]
    inner_mean = factor_row * inner_row / total_width
    unit_rows = rows_buf[0, shard_of(me), :].astype(F32) * factor_row
    shift = unit_rows * inner_mean
    grad_ref[...] = (factor_row * (gain_buf[shard_of(me), :] * sums_last(1) - shift)).astype(BF16)

    for copies in (*gathers, *sums, memory_sends, memory_mates, back_sends, inner_sends):
        for copy in copies.values():
            copy.wait_send()
    back_to_mate.wait_send()


def solution(mesh):
    seq_size, tensor_size = mesh.shape["seq"], mesh.shape["tensor"]

    def local(
        inputs,
        cotangent,
        norm_gain,
        head_gain,
        query_weight,
        key_weight,
        output_weight,
        modality,
        segments,
        block_order,
    ):
        rows, width = inputs.shape
        total_width = width * tensor_size
        heads = query_weight.shape[2] // HEAD_DIM
        vmem = pl.BlockSpec(memory_space=pltpu.VMEM)
        anywhere = pl.BlockSpec(memory_space=pl.ANY)
        dma = pltpu.SemaphoreType.DMA
        shape = jax.ShapeDtypeStruct((width, rows), BF16)
        block = (seq_size, rows, HEAD_DIM)
        attention_out, grad_input = pl.pallas_call(
            functools.partial(kernel, seq_size, tensor_size),
            out_shape=(shape, shape),
            in_specs=[pl.BlockSpec(memory_space=pltpu.SMEM)] + [vmem] * 4 + [anywhere] * 5,
            out_specs=(vmem, vmem),
            scratch_shapes=[
                pltpu.VMEM(query_weight.shape, BF16),
                pltpu.VMEM(key_weight.shape, BF16),
                pltpu.VMEM(output_weight.shape, BF16),
                pltpu.VMEM((2, total_width, rows), BF16),
                pltpu.VMEM((total_width, rows), F32),
                pltpu.VMEM((2, rows, heads * HEAD_DIM), F32),
                pltpu.VMEM((2, rows, HEAD_DIM), F32),
                pltpu.VMEM((2, heads * HEAD_DIM, rows), F32),
                pltpu.VMEM((heads * rows, HEAD_DIM), F32),
                pltpu.VMEM((rows, HEAD_DIM), F32),
                pltpu.VMEM((2, *block), BF16),
                pltpu.VMEM((heads * rows, HEAD_DIM), BF16),
                pltpu.VMEM((2, 4, 2, width, rows), BF16),
                pltpu.VMEM((2, 4, width, rows), BF16),
                pltpu.VMEM((2, 2, width // 2, rows), BF16),
                pltpu.VMEM((2, 3, width, rows), BF16),
                pltpu.VMEM((2, 2, width, rows), BF16),
                pltpu.VMEM((2, *block), BF16),
                pltpu.VMEM(block, BF16),
                pltpu.VMEM(block, BF16),
                pltpu.VMEM(block, BF16),
                pltpu.VMEM((4, 2 * width, rows), F32),
                pltpu.VMEM((8, rows), F32),
                pltpu.VMEM((tensor_size, 8, rows), F32),
                dma((5,)),
                dma((2, 10)),
                dma((2, 10)),
                dma((2, seq_size)),
                dma((2, seq_size)),
                dma((2, 10)),
                dma((2, 10)),
                dma((seq_size,)),
                dma((seq_size,)),
                dma((tensor_size,)),
                dma((tensor_size,)),
            ],
            compiler_params=pltpu.CompilerParams(collective_id=0, has_side_effects=True),
        )(
            block_order,
            modality.reshape(1, rows),
            segments.reshape(seq_size, rows),
            norm_gain,
            head_gain,
            inputs.T,
            cotangent.T,
            query_weight,
            key_weight,
            output_weight,
        )
        return attention_out.T, grad_input.T

    return jax.shard_map(
        local,
        mesh=mesh,
        in_specs=(
            P(("dp", "seq"), "tensor"),
            P(("dp", "seq"), "tensor"),
            P(),
            P(),
            P(None, None, "tensor"),
            P(None, None, "tensor"),
            P(None, "tensor", None),
            P(("dp", "seq")),
            P("dp"),
            P("dp"),
        ),
        out_specs=(P(("dp", "seq"), "tensor"), P(("dp", "seq"), "tensor")),
        check_vma=False,
    )
```

```python
import functools
import math

import jax
import jax.numpy as jnp
from jax import lax
from jax.experimental import pallas as pl
from jax.experimental.pallas import tpu as pltpu
from jax.sharding import PartitionSpec as P

HEAD_DIM = 128
EPSILON = 1e-06
MESH = pl.DeviceIdType.MESH
F32 = jnp.float32
BF16 = jnp.bfloat16

FAR, RIGHT, LEFT, OWN = range(4)


def dot(a, b):
    return jnp.dot(a, b, preferred_element_type=F32)


def dot_nt(a, b):
    return lax.dot_general(a, b, (((1,), (1,)), ((), ())), preferred_element_type=F32)


def dot_tn(a, b):
    return lax.dot_general(a, b, (((0,), (0,)), ((), ())), preferred_element_type=F32)


def remote(src, dst, send_sem, recv_sem, **device):
    return pltpu.make_async_remote_copy(
        src_ref=src,
        dst_ref=dst,
        send_sem=send_sem,
        recv_sem=recv_sem,
        device_id=device,
        device_id_type=MESH,
    )


def kernel(
    seq_size,
    tensor_size,
    order_hbm,
    modality_hbm,
    segments_hbm,
    norm_gain_hbm,
    head_gain_hbm,
    inputs_ref,
    cotangent_ref,
    query_hbm,
    key_hbm,
    output_hbm,
    attention_ref,
    grad_ref,
    order_ref,
    modality_ref,
    segments_ref,
    norm_gain_ref,
    head_gain_ref,
    query_w,
    key_w,
    output_w,
    rows_buf,
    gain_buf,
    query_acc,
    key_acc,
    back_acc,
    query_raw_buf,
    key_raw_buf,
    memory_buf,
    back_buf,
    sums_stage,
    sums_mate,
    sums_hop,
    sums_out,
    sums_final,
    memory_back,
    memory_mate,
    memory_out,
    memory_in,
    partial_buf,
    inner_out,
    inner_in,
    local_sem,
    gather_send,
    gather_recv,
    memory_send,
    memory_recv,
    sums_send,
    sums_recv,
    mate_send,
    mate_recv,
    back_send,
    back_recv,
    inner_send,
    inner_recv,
):
    seq = lax.axis_index("seq")
    me = lax.axis_index("tensor")
    core = lax.rem(me, 2)
    mate = me + 1 - 2 * core
    right = lax.rem(me + 2, tensor_size)
    left = lax.rem(me + tensor_size - 2, tensor_size)
    far = lax.rem(me + 4, tensor_size)
    width, rows = inputs_ref.shape
    half = width // 2
    total_width = width * tensor_size
    scale = 1.0 / math.sqrt(HEAD_DIM)
    half_a, half_b = pl.ds(0, half), pl.ds(half, half)

    barrier = pltpu.get_barrier_semaphore()
    for step in range(1, tensor_size):
        pl.semaphore_signal(
            barrier, inc=1, device_id={"tensor": lax.rem(me + step, tensor_size)}, device_id_type=MESH
        )
    for step in range(1, seq_size):
        pl.semaphore_signal(
            barrier, inc=1, device_id={"seq": lax.rem(seq + step, seq_size)}, device_id_type=MESH
        )

    def shard_of(slot, part=0, size=width):
        return pl.ds(pl.multiple_of(slot * width + part * half, 32), size)

    def chip_of(slot):
        return pl.ds(pl.multiple_of((slot - core) * width, 2 * width), 2 * width)

    loads = [
        pltpu.make_async_copy(src, dst, local_sem.at[k])
        for k, (src, dst) in enumerate(
            (
                (modality_hbm, modality_ref),
                (norm_gain_hbm, norm_gain_ref),
                (head_gain_hbm, head_gain_ref),
                (segments_hbm, segments_ref),
                (order_hbm, order_ref),
                (inputs_ref, rows_buf.at[0, shard_of(me)]),
                (query_hbm, query_w),
                (key_hbm, key_w),
                (output_hbm, output_w),
                (cotangent_ref, rows_buf.at[1, shard_of(me)]),
            )
        )
    ]
    for copy in loads:
        copy.start()
    with jax.named_scope("barrier"):
        pl.semaphore_wait(barrier, tensor_size - 1 + seq_size - 1)

    def gather(k):
        own = (inputs_ref, cotangent_ref)[k]
        copies = {}

        def add(name, which, part, device, from_input=False):
            there = rows_buf.at[k, shard_of(which, part, half)]
            here = own.at[pl.ds(part * half, half)] if from_input else there
            index = len(copies)
            copies[name] = remote(here, there, gather_send.at[k, index], gather_recv.at[k, index], tensor=device)

        for part, letter in enumerate("ab"):
            add("left_" + letter, me, part, right, True)
            add("right_" + letter, me, part, left, True)
            add("mate_own_" + letter, me, part, mate, True)
            add("mate_left_" + letter, left, part, mate)
            add("mate_right_" + letter, right, part, mate)
            add("mate_far_" + letter, far, part, mate)
        add("far_a", left, 0, right)
        add("far_b", right, 1, left)
        return copies

    gathers = [gather(0), gather(1)]

    def gather_start(k):
        for name in ("left_a", "right_b", "mate_own_a", "mate_own_b"):
            gathers[k][name].start()

    def gather_rest(k):
        for name in ("left_b", "right_a"):
            gathers[k][name].start()

    def gather_first(k):
        copies = gathers[k]
        copies["left_a"].wait_recv()
        copies["far_a"].start()
        copies["mate_left_a"].start()
        copies["right_b"].wait_recv()
        copies["far_b"].start()
        copies["mate_right_b"].start()

    def gather_near(k):
        copies = gathers[k]
        copies["left_b"].wait_recv()
        copies["mate_left_b"].start()
        copies["right_a"].wait_recv()
        copies["mate_right_a"].start()

    def gather_far(k):
        copies = gathers[k]
        copies["far_a"].wait_recv()
        copies["mate_far_a"].start()
        copies["far_b"].wait_recv()
        copies["mate_far_b"].start()

    def from_mate(k, name):
        for letter in "ab":
            gathers[k]["mate_" + name + "_" + letter].wait_recv()

    gather_start(0)
    gather_rest(0)

    row_of = lax.broadcasted_iota(jnp.int32, (rows, rows), 0)
    col_of = lax.broadcasted_iota(jnp.int32, (rows, rows), 1)
    diagonal = row_of == col_of

    def as_column(row):
        return jnp.sum(jnp.where(diagonal, row, 0.0), axis=1, keepdims=True)

    def as_row(column):
        return jnp.sum(jnp.where(diagonal, column, 0.0), axis=0, keepdims=True)

    for copy in loads[:5]:
        copy.wait()
    image_row = (modality_ref[...] == 1).astype(F32)
    is_image = as_column(image_row) > 0.5
    image_pick = jnp.broadcast_to(is_image, (rows, HEAD_DIM))
    image_pick_t = jnp.broadcast_to(image_row > 0.5, (HEAD_DIM, rows))
    with jax.named_scope("gains"):
        for k in range(total_width // HEAD_DIM):
            columns = slice(k * HEAD_DIM, (k + 1) * HEAD_DIM)
            gain_buf[columns, :] = jnp.where(image_pick, norm_gain_ref[1:2, columns], norm_gain_ref[0:1, columns]).T

    def segments_of(block):
        return segments_ref[pl.ds(order_ref[block], 1), :].astype(F32)

    heads = query_acc.shape[2] // HEAD_DIM
    depth = heads * HEAD_DIM
    key_segments = jnp.concatenate([segments_of(k) for k in range(seq_size)], axis=1)
    query_segments = jnp.concatenate([as_column(segments_of(seq))] * heads, axis=0)
    query_acc[...] = jnp.zeros_like(query_acc)
    key_acc[...] = jnp.zeros_like(key_acc)
    back_acc[...] = jnp.zeros_like(back_acc)

    def project(slot, squares):
        span = chip_of(slot)
        x = rows_buf[0, span, :].astype(F32)
        scaled = (x * gain_buf[span, :]).T.astype(BF16)
        for e in range(2):
            query_acc[e] += dot(scaled, query_w[e, span, :])
            key_acc[e] += dot(scaled, key_w[e, span, :])
        return squares + jnp.sum(x * x, axis=0, keepdims=True)

    squares = jnp.zeros((1, rows), F32)
    with jax.named_scope("gather_first"):
        gather_first(0)
        gather_start(1)
        for copy in loads[5:8]:
            copy.wait()
        from_mate(0, "own")
    with jax.named_scope("project_own"):
        squares = project(me, squares)
    with jax.named_scope("gather_near"):
        gather_near(0)
        from_mate(0, "left")
    with jax.named_scope("project_left"):
        squares = project(left, squares)
    with jax.named_scope("gather_right"):
        from_mate(0, "right")
    with jax.named_scope("project_right"):
        squares = project(right, squares)
    with jax.named_scope("gather_far"):
        gather_far(0)
    with jax.named_scope("gather_far_mate"):
        from_mate(0, "far")
    with jax.named_scope("project_far"):
        squares = project(far, squares)

    factor_row = lax.rsqrt(squares / total_width + EPSILON)
    row_factor = as_column(factor_row)

    def picked(acc, columns):
        return jnp.where(image_pick, acc[1, :, columns], acc[0, :, columns]) * row_factor

    def head_factor(raw):
        return lax.rsqrt(jnp.mean(raw * raw, axis=-1, keepdims=True) + EPSILON)

    def head_gain(kind):
        return jnp.where(image_pick, head_gain_ref[1, kind : kind + 1, :], head_gain_ref[0, kind : kind + 1, :])

    key_raw = picked(key_acc, slice(None))
    key_raw_buf[...] = key_raw
    key_normed = key_raw * head_factor(key_raw) * head_gain(1)
    memory_buf[core, seq] = jnp.where(core == 0, key_normed, key_raw).astype(BF16)

    pair = seq + 1 - 2 * lax.rem(seq, 2)
    turns = sorted(range(2, seq_size, 2), key=lambda step: -min(step, seq_size - step))
    all_steps = sorted(range(1, seq_size), key=lambda step: -min(step, seq_size - step))
    memory_copies = {}

    def memory_add(name, block, device):
        index = len(memory_copies)
        ref = memory_buf.at[core, block]
        memory_copies[name] = remote(ref, ref, memory_send.at[index], memory_recv.at[index], **device)

    memory_add("pair", seq, {"seq": pair})
    arrivals = [(seq, None, ("mate", "own", 0)), (pair, ("pair"), ("mate", "pair", 0))]
    for name, block in (("own", seq), ("pair", pair)):
        memory_add(("mate", name, 0), block, {"tensor": mate})
        for turn in turns:
            memory_add((name, turn), block, {"seq": lax.rem(seq + turn, seq_size)})
            behind = lax.rem(block + seq_size - turn, seq_size)
            memory_add(("mate", name, turn), behind, {"tensor": mate})
            arrivals.append((behind, (name, turn), ("mate", name, turn)))
    arrivals = arrivals[:1] + arrivals[2 : 2 + len(turns)] + arrivals[1:2] + arrivals[2 + len(turns) :]

    with jax.named_scope("memory_start"):
        memory_copies["pair"].start()
        for turn in turns:
            memory_copies["own", turn].start()
        memory_copies["mate", "own", 0].start()

    with jax.named_scope("cot_first"):
        gather_first(1)
        gather_rest(1)

    with jax.named_scope("pair_wait"):
        memory_copies["pair"].wait_recv()
        for turn in turns:
            memory_copies["pair", turn].start()
        memory_copies["mate", "pair", 0].start()

    with jax.named_scope("query_norm"):
        for h in range(heads):
            raw = picked(query_acc, slice(h * HEAD_DIM, (h + 1) * HEAD_DIM))
            query_raw_buf[h * rows : (h + 1) * rows] = raw
        query_gain = jnp.concatenate([head_gain(0)] * heads, axis=0)
        query_raw = query_raw_buf[...]
        query_normed = (query_raw * head_factor(query_raw) * query_gain).astype(BF16)

    def back_project(slot):
        span = chip_of(slot)
        for e in range(2):
            back_acc[e] += dot(output_w[e, :, span], rows_buf[1, span, :])

    with jax.named_scope("cot_own"):
        loads[8].wait()
        loads[9].wait()
        from_mate(1, "own")
        back_project(me)

    with jax.named_scope("memory_wait"):
        for turn in turns:
            memory_copies["own", turn].wait_recv()
            memory_copies["mate", "own", turn].start()
        for turn in turns:
            memory_copies["pair", turn].wait_recv()
            memory_copies["mate", "pair", turn].start()
    with jax.named_scope("cot_far"):
        gather_far(1)
    with jax.named_scope("memory_mate"):
        for _, _, handed in arrivals:
            memory_copies[handed].wait_recv()

    with jax.named_scope("attention"):
        all_rows = seq_size * rows
        keys = memory_buf[0].reshape(all_rows, HEAD_DIM)
        values = memory_buf[1].reshape(all_rows, HEAD_DIM)
        scores = dot_nt(query_normed, keys) * scale
        weights = jnp.where(key_segments <= query_segments, jnp.exp(scores), 0.0).astype(BF16)
        denominator = jnp.sum(weights.astype(F32), axis=1, keepdims=True)
        attended = (dot(weights, values) / denominator).astype(BF16)
    with jax.named_scope("cot_near"):
        gather_near(1)

    places = {FAR: far, RIGHT: right, LEFT: left, OWN: me}

    def by_expert(parts, picks, axis):
        zero = jnp.zeros_like(parts)
        return jnp.concatenate(
            [jnp.where(picks, zero, parts), jnp.where(picks, parts, zero)], axis=axis
        ).astype(BF16)

    def sums_copies(k):
        def to(slot, src, dst, device):
            return remote(src, dst, sums_send.at[k, slot], sums_recv.at[k, slot], tensor=device)

        copies = {("mate", p): to(p, sums_stage.at[k, p, 1 - core], sums_mate.at[k, p], mate) for p in range(4)}
        copies["far_a"] = to(4, sums_out.at[k, FAR, half_a], sums_hop.at[k, 0], right)
        copies["far_b"] = to(5, sums_out.at[k, FAR, half_b], sums_hop.at[k, 1], left)
        copies["right_a"] = to(6, sums_out.at[k, RIGHT, half_a], sums_final.at[k, 0, half_a], right)
        copies["right_b"] = to(7, sums_out.at[k, RIGHT, half_b], sums_final.at[k, 0, half_b], right)
        copies["left_a"] = to(8, sums_out.at[k, LEFT, half_a], sums_final.at[k, 1, half_a], left)
        copies["left_b"] = to(9, sums_out.at[k, LEFT, half_b], sums_final.at[k, 1, half_b], left)
        return copies

    sums = [sums_copies(0), sums_copies(1)]

    def chip_sum(k, place, part=slice(None)):
        return sums_stage[k, place, core, part].astype(F32) + sums_mate[k, place, part].astype(F32)

    def sums_first(k):
        copies = sums[k]
        copies["mate", FAR].wait_recv()
        sums_out[k, FAR] = chip_sum(k, FAR).astype(BF16)
        copies["far_a"].start()
        copies["far_b"].start()

    def sums_second(k):
        copies = sums[k]
        for place, name, part in ((RIGHT, "right_b", half_b), (LEFT, "left_a", half_a)):
            copies["mate", place].wait_recv()
            sums_out[k, place, part] = chip_sum(k, place, part).astype(BF16)
            copies[name].start()

    def sums_third(k):
        copies = sums[k]
        for place, hop, name, part in ((RIGHT, 0, "far_a", half_a), (LEFT, 1, "far_b", half_b)):
            copies[name].wait_recv()
            sums_out[k, place, part] = (chip_sum(k, place, part) + sums_hop[k, hop].astype(F32)).astype(BF16)
            copies["right_a" if place == RIGHT else "left_b"].start()

    def sums_last(k):
        copies = sums[k]
        copies["mate", OWN].wait_recv()
        for name in ("right_b", "left_a", "right_a", "left_b"):
            copies[name].wait_recv()
        return chip_sum(k, OWN) + sums_final[k, 0].astype(F32) + sums_final[k, 1].astype(F32)

    head_rows = [slice(h * rows, (h + 1) * rows) for h in range(heads)]

    def side_by_side(stacked):
        return jnp.concatenate([stacked[r] for r in head_rows], axis=1)

    with jax.named_scope("out_project"):
        wide_pick = jnp.broadcast_to(is_image, (rows, depth))
        attended_parts = by_expert(side_by_side(attended.astype(F32)), wide_pick, 1)
        for place in (FAR, RIGHT, LEFT, OWN):
            span = chip_of(places[place])
            block = dot(attended_parts[:, :depth], output_w[0, :, span]) + dot(
                attended_parts[:, depth:], output_w[1, :, span]
            )
            sums_stage[0, place] = block.T.astype(BF16).reshape(2, width, rows)
            sums[0]["mate", place].start()

    with jax.named_scope("sums0_first"):
        sums_first(0)
    with jax.named_scope("cot_project"):
        from_mate(1, "far")
        back_project(far)
        from_mate(1, "left")
        back_project(left)
        from_mate(1, "right")
        back_project(right)

    with jax.named_scope("back_scores"):
        for h in range(heads):
            columns = slice(h * HEAD_DIM, (h + 1) * HEAD_DIM)
            back_buf[head_rows[h]] = jnp.where(
                image_pick_t, back_acc[1, columns, :], back_acc[0, columns, :]
            ).T.astype(BF16)
        back_attended = back_buf[...]
        offset = jnp.sum(back_attended.astype(F32) * attended.astype(F32), axis=1, keepdims=True)

    far_first = [block for block, _, (_, name, turn) in sorted(arrivals, key=lambda a: (-min(a[2][2], seq_size - a[2][2]), -len(a[2][1])))]
    mate_copies, back_copies = [], []
    for index, block in enumerate(far_first):
        mate_copies.append(
            remote(
                memory_back.at[1 - core, block],
                memory_mate.at[index],
                mate_send.at[index],
                mate_recv.at[index],
                tensor=mate,
            )
        )
        back_copies.append(
            remote(memory_out.at[index], memory_in.at[index], back_send.at[index], back_recv.at[index], seq=block)
        )
    last = seq_size - 1
    back_copies.pop(last)
    with jax.named_scope("back_attention"):
        probability = (weights.astype(F32) / denominator).astype(BF16)
        back_probability = dot_nt(back_attended, values)
        back_score = (probability.astype(F32) * (back_probability - offset)).astype(BF16)
        memory_back[0] = (dot_tn(back_score, query_normed) * scale).astype(BF16).reshape(seq_size, rows, HEAD_DIM)
        memory_back[1] = dot_tn(probability, back_attended).astype(BF16).reshape(seq_size, rows, HEAD_DIM)
        for copy in mate_copies:
            copy.start()

    with jax.named_scope("back_send"):
        for index, block in enumerate(far_first):
            mate_copies[index].wait_recv()
            both = memory_back[core, block].astype(F32) + memory_mate[index].astype(F32)
            if index == last:
                slice_grad = both
            else:
                memory_out[index] = both.astype(BF16)
                back_copies[index].start()

    with jax.named_scope("sums0_second"):
        sums_second(0)

    with jax.named_scope("query_back"):
        back_query = dot(back_score, keys)
        query_factor = head_factor(query_raw)
        query_unit = query_raw * query_factor
        weighted = query_gain * (back_query * scale)
        query_back = query_factor * (
            weighted - query_unit * jnp.mean(weighted * query_unit, axis=-1, keepdims=True)
        )
        query_back = query_back.astype(BF16).astype(F32)
        inner = jnp.sum(side_by_side(query_back * query_raw), axis=1, keepdims=True)
        back_columns = jnp.concatenate([query_back[r].T for r in head_rows], axis=0)
        query_parts = by_expert(back_columns, jnp.concatenate([image_pick_t] * heads, axis=0), 0)
        for place in (FAR, RIGHT, LEFT, OWN):
            span = chip_of(places[place])
            partial_buf[place] = dot(query_w[0, span, :], query_parts[:depth]) + dot(
                query_w[1, span, :], query_parts[depth:]
            )

    with jax.named_scope("sums0_third"):
        sums_third(0)

    with jax.named_scope("back_wait"):
        for index, copy in enumerate(back_copies):
            copy.wait_recv()
            slice_grad = slice_grad + memory_in[index].astype(F32)
    key_raw = key_raw_buf[...]
    key_factor = head_factor(key_raw)
    key_unit = key_raw * key_factor
    weighted = head_gain(1) * slice_grad
    key_back = key_factor * (weighted - key_unit * jnp.mean(weighted * key_unit, axis=-1, keepdims=True))
    slice_back = jnp.where(core == 0, key_back, slice_grad).astype(BF16).astype(F32)
    slice_parts = by_expert(slice_back.T, image_pick_t, 0)

    inner = inner + jnp.sum(slice_back * key_raw, axis=1, keepdims=True)
    inner_row = as_row(inner)
    inner_out[...] = jnp.broadcast_to(inner_row, inner_out.shape)
    inner_sends = {}
    for step in range(1, tensor_size):
        inner_sends[step] = remote(
            inner_out,
            inner_in.at[step],
            inner_send.at[step],
            inner_recv.at[step],
            tensor=lax.rem(me + step, tensor_size),
        )
        inner_sends[step].start()

    with jax.named_scope("key_back"):
        for place in (FAR, RIGHT, LEFT, OWN):
            span = chip_of(places[place])
            part = (
                partial_buf[place]
                + dot(key_w[0, span, :], slice_parts[:HEAD_DIM])
                + dot(key_w[1, span, :], slice_parts[HEAD_DIM:])
            )
            sums_stage[1, place] = part.astype(BF16).reshape(2, width, rows)
            sums[1]["mate", place].start()
    with jax.named_scope("sums1_first"):
        sums_first(1)
    with jax.named_scope("sums1_second"):
        sums_second(1)
    with jax.named_scope("sums0_last"):
        attention_ref[...] = sums_last(0).astype(BF16)
    with jax.named_scope("sums1_third"):
        sums_third(1)
    with jax.named_scope("inner_wait"):
        for step in range(1, tensor_size):
            inner_sends[step].wait_recv()
            inner_row = inner_row + inner_in[step, 0:1, :]
    inner_mean = inner_row / total_width
    unit_rows = rows_buf[0, shard_of(me), :].astype(F32) * factor_row
    with jax.named_scope("sums1_last"):
        shift = unit_rows * inner_mean
        grad_ref[...] = (factor_row * (gain_buf[shard_of(me), :] * sums_last(1) - shift)).astype(BF16)

    with jax.named_scope("drain"):
        for copies in (*gathers, *sums, memory_copies, inner_sends):
            for copy in copies.values():
                copy.wait_send()
        for copy in (*mate_copies, *back_copies):
            copy.wait_send()


def finish(attention_in, grad_in, attention_ref, grad_ref):
    attention_ref[...] = attention_in[...]
    grad_ref[...] = grad_in[...]


def solution(mesh):
    seq_size, tensor_size = mesh.shape["seq"], mesh.shape["tensor"]

    def local(
        inputs,
        cotangent,
        norm_gain,
        head_gain,
        query_weight,
        key_weight,
        output_weight,
        modality,
        segments,
        block_order,
    ):
        rows, width = inputs.shape
        total_width = width * tensor_size
        heads = query_weight.shape[2] // HEAD_DIM
        vmem = pl.BlockSpec(memory_space=pltpu.VMEM)
        anywhere = pl.BlockSpec(memory_space=pl.ANY)
        dma = pltpu.SemaphoreType.DMA
        shape = jax.ShapeDtypeStruct((width, rows), BF16)
        block = (seq_size, rows, HEAD_DIM)
        attention_out, grad_input = pl.pallas_call(
            functools.partial(kernel, seq_size, tensor_size),
            out_shape=(shape, shape),
            in_specs=[anywhere] * 10,
            out_specs=(vmem, vmem),
            scratch_shapes=[
                pltpu.SMEM(block_order.shape, jnp.int32),
                pltpu.VMEM((1, rows), jnp.int32),
                pltpu.VMEM((seq_size, rows), jnp.int32),
                pltpu.VMEM(norm_gain.shape, F32),
                pltpu.VMEM(head_gain.shape, F32),
                pltpu.VMEM(query_weight.shape, BF16),
                pltpu.VMEM(key_weight.shape, BF16),
                pltpu.VMEM(output_weight.shape, BF16),
                pltpu.VMEM((2, total_width, rows), BF16),
                pltpu.VMEM((total_width, rows), F32),
                pltpu.VMEM((2, rows, heads * HEAD_DIM), F32),
                pltpu.VMEM((2, rows, HEAD_DIM), F32),
                pltpu.VMEM((2, heads * HEAD_DIM, rows), F32),
                pltpu.VMEM((heads * rows, HEAD_DIM), F32),
                pltpu.VMEM((rows, HEAD_DIM), F32),
                pltpu.VMEM((2, *block), BF16),
                pltpu.VMEM((heads * rows, HEAD_DIM), BF16),
                pltpu.VMEM((2, 4, 2, width, rows), BF16),
                pltpu.VMEM((2, 4, width, rows), BF16),
                pltpu.VMEM((2, 2, width // 2, rows), BF16),
                pltpu.VMEM((2, 3, width, rows), BF16),
                pltpu.VMEM((2, 2, width, rows), BF16),
                pltpu.VMEM((2, *block), BF16),
                pltpu.VMEM(block, BF16),
                pltpu.VMEM(block, BF16),
                pltpu.VMEM(block, BF16),
                pltpu.VMEM((4, 2 * width, rows), F32),
                pltpu.VMEM((8, rows), F32),
                pltpu.VMEM((tensor_size, 8, rows), F32),
                dma((10,)),
                dma((2, 14)),
                dma((2, 14)),
                dma((2 * seq_size,)),
                dma((2 * seq_size,)),
                dma((2, 10)),
                dma((2, 10)),
                dma((seq_size,)),
                dma((seq_size,)),
                dma((seq_size,)),
                dma((seq_size,)),
                dma((tensor_size,)),
                dma((tensor_size,)),
            ],
            compiler_params=pltpu.CompilerParams(collective_id=0, has_side_effects=True),
        )(
            block_order,
            modality.reshape(1, rows),
            segments.reshape(seq_size, rows),
            norm_gain,
            head_gain,
            inputs.T,
            cotangent.T,
            query_weight,
            key_weight,
            output_weight,
        )
        attention_out, grad_input = pl.pallas_call(
            finish, out_shape=(shape, shape), in_specs=[vmem, vmem], out_specs=(vmem, vmem)
        )(attention_out, grad_input)
        return attention_out.T, grad_input.T

    return jax.shard_map(
        local,
        mesh=mesh,
        in_specs=(
            P(("dp", "seq"), "tensor"),
            P(("dp", "seq"), "tensor"),
            P(),
            P(),
            P(None, None, "tensor"),
            P(None, None, "tensor"),
            P(None, "tensor", None),
            P(("dp", "seq")),
            P("dp"),
            P("dp"),
        ),
        out_specs=(P(("dp", "seq"), "tensor"), P(("dp", "seq"), "tensor")),
        check_vma=False,
    )
```

```python
import functools
import math

import jax
import jax.numpy as jnp
from jax import lax
from jax.experimental import pallas as pl
from jax.experimental.pallas import tpu as pltpu
from jax.sharding import PartitionSpec as P

HEAD_DIM = 128
EPSILON = 1e-06
MESH = pl.DeviceIdType.MESH
F32 = jnp.float32
BF16 = jnp.bfloat16

FAR, RIGHT, LEFT, OWN = range(4)


def dot(a, b):
    return jnp.dot(a, b, preferred_element_type=F32)


def dot_nt(a, b):
    return lax.dot_general(a, b, (((1,), (1,)), ((), ())), preferred_element_type=F32)


def dot_tn(a, b):
    return lax.dot_general(a, b, (((0,), (0,)), ((), ())), preferred_element_type=F32)


def remote(src, dst, send_sem, recv_sem, **device):
    return pltpu.make_async_remote_copy(
        src_ref=src,
        dst_ref=dst,
        send_sem=send_sem,
        recv_sem=recv_sem,
        device_id=device,
        device_id_type=MESH,
    )


def kernel(
    seq_size,
    tensor_size,
    order_hbm,
    modality_hbm,
    segments_hbm,
    norm_gain_hbm,
    head_gain_hbm,
    inputs_ref,
    cotangent_ref,
    query_hbm,
    key_hbm,
    output_hbm,
    attention_ref,
    grad_ref,
    order_ref,
    modality_ref,
    segments_ref,
    norm_gain_ref,
    head_gain_ref,
    query_w,
    key_w,
    output_w,
    rows_buf,
    gain_buf,
    query_acc,
    key_acc,
    back_acc,
    query_raw_buf,
    key_raw_buf,
    memory_buf,
    back_buf,
    sums_stage,
    sums_mate,
    sums_hop,
    sums_out,
    sums_final,
    memory_back,
    memory_mate,
    memory_out,
    memory_in,
    partial_buf,
    inner_out,
    inner_in,
    local_sem,
    gather_send,
    gather_recv,
    memory_send,
    memory_recv,
    sums_send,
    sums_recv,
    mate_send,
    mate_recv,
    back_send,
    back_recv,
    inner_send,
    inner_recv,
):
    seq = lax.axis_index("seq")
    me = lax.axis_index("tensor")
    core = lax.rem(me, 2)
    mate = me + 1 - 2 * core
    right = lax.rem(me + 2, tensor_size)
    left = lax.rem(me + tensor_size - 2, tensor_size)
    far = lax.rem(me + 4, tensor_size)
    width, rows = inputs_ref.shape
    half = width // 2
    total_width = width * tensor_size
    scale = 1.0 / math.sqrt(HEAD_DIM)
    half_a, half_b = pl.ds(0, half), pl.ds(half, half)

    pair = seq + 1 - 2 * lax.rem(seq, 2)
    turns = sorted(range(2, seq_size, 2), key=lambda step: -min(step, seq_size - step))
    greeted = [{"tensor": mate}, {"tensor": right}, {"tensor": left}, {"seq": pair}]
    greeted += [{"seq": lax.rem(seq + turn, seq_size)} for turn in turns]
    barrier = pltpu.get_barrier_semaphore()
    for device in greeted:
        pl.semaphore_signal(barrier, inc=1, device_id=device, device_id_type=MESH)

    def shard_of(slot, part=0, size=width):
        return pl.ds(pl.multiple_of(slot * width + part * half, 32), size)

    def chip_of(slot):
        return pl.ds(pl.multiple_of((slot - core) * width, 2 * width), 2 * width)

    loads = [
        pltpu.make_async_copy(src, dst, local_sem.at[k])
        for k, (src, dst) in enumerate(
            (
                (modality_hbm, modality_ref),
                (norm_gain_hbm, norm_gain_ref),
                (head_gain_hbm, head_gain_ref),
                (segments_hbm, segments_ref),
                (order_hbm, order_ref),
                (inputs_ref, rows_buf.at[0, shard_of(me)]),
                (query_hbm, query_w),
                (key_hbm, key_w),
                (output_hbm, output_w),
                (cotangent_ref, rows_buf.at[1, shard_of(me)]),
            )
        )
    ]
    for copy in loads:
        copy.start()
    with jax.named_scope("barrier"):
        pl.semaphore_wait(barrier, len(greeted))

    def gather(k):
        own = (inputs_ref, cotangent_ref)[k]
        copies = {}

        def add(name, which, part, device, from_input=False):
            there = rows_buf.at[k, shard_of(which, part, half)]
            here = own.at[pl.ds(part * half, half)] if from_input else there
            index = len(copies)
            copies[name] = remote(here, there, gather_send.at[k, index], gather_recv.at[k, index], tensor=device)

        for part, letter in enumerate("ab"):
            add("left_" + letter, me, part, right, True)
            add("right_" + letter, me, part, left, True)
            add("mate_own_" + letter, me, part, mate, True)
            add("mate_left_" + letter, left, part, mate)
            add("mate_right_" + letter, right, part, mate)
            add("mate_far_" + letter, far, part, mate)
        add("far_a", left, 0, right)
        add("far_b", right, 1, left)
        return copies

    gathers = [gather(0), gather(1)]

    def gather_start(k):
        for name in ("left_a", "right_b", "mate_own_a", "mate_own_b"):
            gathers[k][name].start()

    def gather_rest(k):
        for name in ("left_b", "right_a"):
            gathers[k][name].start()

    def gather_first(k):
        copies = gathers[k]
        copies["left_a"].wait_recv()
        copies["far_a"].start()
        copies["mate_left_a"].start()
        copies["right_b"].wait_recv()
        copies["far_b"].start()
        copies["mate_right_b"].start()

    def gather_near(k):
        copies = gathers[k]
        copies["left_b"].wait_recv()
        copies["mate_left_b"].start()
        copies["right_a"].wait_recv()
        copies["mate_right_a"].start()

    def gather_far(k):
        copies = gathers[k]
        copies["far_a"].wait_recv()
        copies["mate_far_a"].start()
        copies["far_b"].wait_recv()
        copies["mate_far_b"].start()

    def from_mate(k, name):
        for letter in "ab":
            gathers[k]["mate_" + name + "_" + letter].wait_recv()

    gather_start(0)
    gather_rest(0)

    row_of = lax.broadcasted_iota(jnp.int32, (rows, rows), 0)
    col_of = lax.broadcasted_iota(jnp.int32, (rows, rows), 1)
    diagonal = row_of == col_of

    def as_column(row):
        return jnp.sum(jnp.where(diagonal, row, 0.0), axis=1, keepdims=True)

    def as_row(column):
        return jnp.sum(jnp.where(diagonal, column, 0.0), axis=0, keepdims=True)

    for copy in loads[:5]:
        copy.wait()
    image_row = (modality_ref[...] == 1).astype(F32)
    is_image = as_column(image_row) > 0.5
    image_pick = jnp.broadcast_to(is_image, (rows, HEAD_DIM))
    image_pick_t = jnp.broadcast_to(image_row > 0.5, (HEAD_DIM, rows))
    with jax.named_scope("gains"):
        for k in range(total_width // HEAD_DIM):
            columns = slice(k * HEAD_DIM, (k + 1) * HEAD_DIM)
            gain_buf[columns, :] = jnp.where(image_pick, norm_gain_ref[1:2, columns], norm_gain_ref[0:1, columns]).T

    def segments_of(block):
        return segments_ref[pl.ds(order_ref[block], 1), :].astype(F32)

    heads = query_acc.shape[2] // HEAD_DIM
    depth = heads * HEAD_DIM
    key_segments = jnp.concatenate([segments_of(k) for k in range(seq_size)], axis=1)
    query_segments = jnp.concatenate([as_column(segments_of(seq))] * heads, axis=0)
    query_acc[...] = jnp.zeros_like(query_acc)
    key_acc[...] = jnp.zeros_like(key_acc)
    back_acc[...] = jnp.zeros_like(back_acc)

    def scaled_rows(slot):
        span = chip_of(slot)
        x = rows_buf[0, span, :].astype(F32)
        return (x * gain_buf[span, :]).T.astype(BF16), jnp.sum(x * x, axis=0, keepdims=True)

    def project_key(slot, scaled):
        for e in range(2):
            key_acc[e] += dot(scaled, key_w[e, chip_of(slot), :])

    def project_query(slot, scaled):
        for e in range(2):
            query_acc[e] += dot(scaled, query_w[e, chip_of(slot), :])

    def project(slot, squares):
        scaled, more = scaled_rows(slot)
        project_key(slot, scaled)
        project_query(slot, scaled)
        return squares + more

    squares = jnp.zeros((1, rows), F32)
    with jax.named_scope("gather_first"):
        gather_first(0)
        gather_start(1)
        gather_rest(1)
        for copy in loads[5:8]:
            copy.wait()
        from_mate(0, "own")
    with jax.named_scope("project_own"):
        squares = project(me, squares)
    with jax.named_scope("gather_near"):
        gather_near(0)
        from_mate(0, "left")
    with jax.named_scope("project_left"):
        squares = project(left, squares)
    with jax.named_scope("gather_right"):
        from_mate(0, "right")
    with jax.named_scope("project_right"):
        squares = project(right, squares)
    with jax.named_scope("gather_far"):
        gather_far(0)
    with jax.named_scope("gather_far_mate"):
        from_mate(0, "far")
    with jax.named_scope("project_far"):
        far_scaled, more = scaled_rows(far)
        squares = squares + more
        project_key(far, far_scaled)

    factor_row = lax.rsqrt(squares / total_width + EPSILON)
    row_factor = as_column(factor_row)

    def picked(acc, columns):
        return jnp.where(image_pick, acc[1, :, columns], acc[0, :, columns]) * row_factor

    def head_factor(raw):
        return lax.rsqrt(jnp.mean(raw * raw, axis=-1, keepdims=True) + EPSILON)

    def head_gain(kind):
        return jnp.where(image_pick, head_gain_ref[1, kind : kind + 1, :], head_gain_ref[0, kind : kind + 1, :])

    key_raw = picked(key_acc, slice(None))
    key_raw_buf[...] = key_raw
    key_normed = key_raw * head_factor(key_raw) * head_gain(1)
    memory_buf[core, seq] = jnp.where(core == 0, key_normed, key_raw).astype(BF16)

    memory_copies = {}

    def memory_add(name, block, device):
        index = len(memory_copies)
        ref = memory_buf.at[core, block]
        memory_copies[name] = remote(ref, ref, memory_send.at[index], memory_recv.at[index], **device)

    memory_add("pair", seq, {"seq": pair})
    arrivals = [(seq, None, ("mate", "own", 0)), (pair, ("pair"), ("mate", "pair", 0))]
    for name, block in (("own", seq), ("pair", pair)):
        memory_add(("mate", name, 0), block, {"tensor": mate})
        for turn in turns:
            memory_add((name, turn), block, {"seq": lax.rem(seq + turn, seq_size)})
            behind = lax.rem(block + seq_size - turn, seq_size)
            memory_add(("mate", name, turn), behind, {"tensor": mate})
            arrivals.append((behind, (name, turn), ("mate", name, turn)))
    arrivals = arrivals[:1] + arrivals[2 : 2 + len(turns)] + arrivals[1:2] + arrivals[2 + len(turns) :]

    with jax.named_scope("memory_start"):
        memory_copies["pair"].start()
        for turn in turns:
            memory_copies["own", turn].start()
        memory_copies["mate", "own", 0].start()

    with jax.named_scope("project_query"):
        project_query(far, far_scaled)
    with jax.named_scope("cot_first"):
        gather_first(1)

    with jax.named_scope("pair_wait"):
        memory_copies["pair"].wait_recv()
        for turn in turns:
            memory_copies["pair", turn].start()
        memory_copies["mate", "pair", 0].start()

    with jax.named_scope("query_norm"):
        for h in range(heads):
            raw = picked(query_acc, slice(h * HEAD_DIM, (h + 1) * HEAD_DIM))
            query_raw_buf[h * rows : (h + 1) * rows] = raw
        query_gain = jnp.concatenate([head_gain(0)] * heads, axis=0)
        query_raw = query_raw_buf[...]
        query_normed = (query_raw * head_factor(query_raw) * query_gain).astype(BF16)

    def back_project(slot):
        span = chip_of(slot)
        for e in range(2):
            back_acc[e] += dot(output_w[e, :, span], rows_buf[1, span, :])

    with jax.named_scope("cot_own"):
        loads[8].wait()
        loads[9].wait()
        from_mate(1, "own")
        back_project(me)

    with jax.named_scope("memory_own"):
        for turn in turns:
            memory_copies["own", turn].wait_recv()
            memory_copies["mate", "own", turn].start()
    with jax.named_scope("cot_near"):
        gather_near(1)
    with jax.named_scope("cot_project"):
        from_mate(1, "left")
        back_project(left)
        from_mate(1, "right")
        back_project(right)
    with jax.named_scope("cot_far"):
        gather_far(1)
    with jax.named_scope("memory_pair"):
        for turn in turns:
            memory_copies["pair", turn].wait_recv()
            memory_copies["mate", "pair", turn].start()
    with jax.named_scope("cot_far_project"):
        from_mate(1, "far")
        back_project(far)
        head_rows = [slice(h * rows, (h + 1) * rows) for h in range(heads)]
        for h in range(heads):
            columns = slice(h * HEAD_DIM, (h + 1) * HEAD_DIM)
            back_buf[head_rows[h]] = jnp.where(
                image_pick_t, back_acc[1, columns, :], back_acc[0, columns, :]
            ).T.astype(BF16)
        back_attended = back_buf[...]
    with jax.named_scope("memory_mate"):
        for _, _, handed in arrivals:
            memory_copies[handed].wait_recv()

    with jax.named_scope("attention"):
        all_rows = seq_size * rows
        keys = memory_buf[0].reshape(all_rows, HEAD_DIM)
        values = memory_buf[1].reshape(all_rows, HEAD_DIM)
        scores = dot_nt(query_normed, keys) * scale
        weights = jnp.where(key_segments <= query_segments, jnp.exp(scores), 0.0).astype(BF16)
        denominator = jnp.sum(weights.astype(F32), axis=1, keepdims=True)
        attended = (dot(weights, values) / denominator).astype(BF16)
    places = {FAR: far, RIGHT: right, LEFT: left, OWN: me}

    def by_expert(parts, picks, axis):
        zero = jnp.zeros_like(parts)
        return jnp.concatenate(
            [jnp.where(picks, zero, parts), jnp.where(picks, parts, zero)], axis=axis
        ).astype(BF16)

    def sums_copies(k):
        def to(slot, src, dst, device):
            return remote(src, dst, sums_send.at[k, slot], sums_recv.at[k, slot], tensor=device)

        copies = {("mate", p): to(p, sums_stage.at[k, p, 1 - core], sums_mate.at[k, p], mate) for p in range(4)}
        copies["far_a"] = to(4, sums_out.at[k, FAR, half_a], sums_hop.at[k, 0], right)
        copies["far_b"] = to(5, sums_out.at[k, FAR, half_b], sums_hop.at[k, 1], left)
        copies["right_a"] = to(6, sums_out.at[k, RIGHT, half_a], sums_final.at[k, 0, half_a], right)
        copies["right_b"] = to(7, sums_out.at[k, RIGHT, half_b], sums_final.at[k, 0, half_b], right)
        copies["left_a"] = to(8, sums_out.at[k, LEFT, half_a], sums_final.at[k, 1, half_a], left)
        copies["left_b"] = to(9, sums_out.at[k, LEFT, half_b], sums_final.at[k, 1, half_b], left)
        return copies

    sums = [sums_copies(0), sums_copies(1)]

    def chip_sum(k, place, part=slice(None)):
        return sums_stage[k, place, core, part].astype(F32) + sums_mate[k, place, part].astype(F32)

    def sums_first(k):
        copies = sums[k]
        copies["mate", FAR].wait_recv()
        sums_out[k, FAR] = chip_sum(k, FAR).astype(BF16)
        copies["far_a"].start()
        copies["far_b"].start()

    def sums_second(k):
        copies = sums[k]
        for place, name, part in ((RIGHT, "right_b", half_b), (LEFT, "left_a", half_a)):
            copies["mate", place].wait_recv()
            sums_out[k, place, part] = chip_sum(k, place, part).astype(BF16)
            copies[name].start()

    def sums_third(k):
        copies = sums[k]
        for place, hop, name, part in ((RIGHT, 0, "far_a", half_a), (LEFT, 1, "far_b", half_b)):
            copies[name].wait_recv()
            sums_out[k, place, part] = (chip_sum(k, place, part) + sums_hop[k, hop].astype(F32)).astype(BF16)
            copies["right_a" if place == RIGHT else "left_b"].start()

    def sums_last(k):
        copies = sums[k]
        copies["mate", OWN].wait_recv()
        for name in ("right_b", "left_a", "right_a", "left_b"):
            copies[name].wait_recv()
        return chip_sum(k, OWN) + sums_final[k, 0].astype(F32) + sums_final[k, 1].astype(F32)

    def side_by_side(stacked):
        return jnp.concatenate([stacked[r] for r in head_rows], axis=1)

    wide_pick = jnp.broadcast_to(is_image, (rows, depth))
    attended_parts = by_expert(side_by_side(attended.astype(F32)), wide_pick, 1)

    def out_project(place):
        span = chip_of(places[place])
        block = dot(attended_parts[:, :depth], output_w[0, :, span]) + dot(
            attended_parts[:, depth:], output_w[1, :, span]
        )
        sums_stage[0, place] = block.T.astype(BF16).reshape(2, width, rows)
        sums[0]["mate", place].start()

    with jax.named_scope("out_far"):
        out_project(FAR)
    with jax.named_scope("back_scores"):
        offset = jnp.sum(back_attended.astype(F32) * attended.astype(F32), axis=1, keepdims=True)

    outgoing = [("pair", turn, lax.rem(pair + turn, seq_size)) for turn in turns]
    outgoing += [("own", turn, lax.rem(seq + turn, seq_size)) for turn in turns]
    outgoing += [("pair", 0, pair), ("own", 0, seq)]
    mate_copies, back_copies = {}, {}
    for index, (name, turn, block) in enumerate(outgoing):
        mate_copies[index] = remote(
            memory_back.at[1 - core, block],
            memory_mate.at[index],
            mate_send.at[index],
            mate_recv.at[index],
            tensor=mate,
        )
        target = lax.rem(seq + turn, seq_size)
        if turn > 0 or name == "pair":
            back_copies[name, turn] = remote(
                memory_out.at[index],
                memory_in.at[index],
                back_send.at[index],
                back_recv.at[index],
                seq=target if turn > 0 else pair,
            )
    in_slot = {(name, turn): index for index, (name, turn, _) in enumerate(outgoing)}
    with jax.named_scope("back_attention"):
        probability = (weights.astype(F32) / denominator).astype(BF16)
        back_probability = dot_nt(back_attended, values)
        back_score = (probability.astype(F32) * (back_probability - offset)).astype(BF16)
        memory_back[0] = (dot_tn(back_score, query_normed) * scale).astype(BF16).reshape(seq_size, rows, HEAD_DIM)
        memory_back[1] = dot_tn(probability, back_attended).astype(BF16).reshape(seq_size, rows, HEAD_DIM)
        for copy in mate_copies.values():
            copy.start()

    with jax.named_scope("sums0_first"):
        sums_first(0)
    with jax.named_scope("out_rest"):
        for place in (RIGHT, LEFT):
            out_project(place)

    with jax.named_scope("back_send"):
        kept = {}
        for index, (name, turn, block) in enumerate(outgoing):
            mate_copies[index].wait_recv()
            both = memory_back[core, block].astype(F32) + memory_mate[index].astype(F32)
            if turn > 0:
                memory_out[index] = both.astype(BF16)
                back_copies[name, turn].start()
            else:
                kept[name] = both

    with jax.named_scope("sums0_second"):
        out_project(OWN)
        sums_second(0)

    with jax.named_scope("query_back"):
        back_query = dot(back_score, keys)
        query_factor = head_factor(query_raw)
        query_unit = query_raw * query_factor
        weighted = query_gain * (back_query * scale)
        query_back = query_factor * (
            weighted - query_unit * jnp.mean(weighted * query_unit, axis=-1, keepdims=True)
        )
        query_back = query_back.astype(BF16).astype(F32)
        inner = jnp.sum(side_by_side(query_back * query_raw), axis=1, keepdims=True)
        back_columns = jnp.concatenate([query_back[r].T for r in head_rows], axis=0)
        query_parts = by_expert(back_columns, jnp.concatenate([image_pick_t] * heads, axis=0), 0)
        for place in (FAR, RIGHT, LEFT, OWN):
            span = chip_of(places[place])
            partial_buf[place] = dot(query_w[0, span, :], query_parts[:depth]) + dot(
                query_w[1, span, :], query_parts[depth:]
            )

    with jax.named_scope("back_wait"):
        def received(name):
            total = kept[name]
            for turn in turns:
                back_copies[name, turn].wait_recv()
                total = total + memory_in[in_slot[name, turn]].astype(F32)
            return total

        memory_out[in_slot["pair", 0]] = received("pair").astype(BF16)
        back_copies["pair", 0].start()
    with jax.named_scope("sums0_third"):
        sums_third(0)
    with jax.named_scope("back_pair_wait"):
        slice_grad = received("own")
        back_copies["pair", 0].wait_recv()
        slice_grad = slice_grad + memory_in[in_slot["pair", 0]].astype(F32)
    key_raw = key_raw_buf[...]
    key_factor = head_factor(key_raw)
    key_unit = key_raw * key_factor
    weighted = head_gain(1) * slice_grad
    key_back = key_factor * (weighted - key_unit * jnp.mean(weighted * key_unit, axis=-1, keepdims=True))
    slice_back = jnp.where(core == 0, key_back, slice_grad).astype(BF16).astype(F32)
    slice_parts = by_expert(slice_back.T, image_pick_t, 0)

    inner = inner + jnp.sum(slice_back * key_raw, axis=1, keepdims=True)
    inner_row = as_row(inner)
    inner_out[...] = jnp.broadcast_to(inner_row, inner_out.shape)
    inner_sends = {}
    for step in range(1, tensor_size):
        inner_sends[step] = remote(
            inner_out,
            inner_in.at[step],
            inner_send.at[step],
            inner_recv.at[step],
            tensor=lax.rem(me + step, tensor_size),
        )
        inner_sends[step].start()

    with jax.named_scope("key_back"):
        for place in (FAR, RIGHT, LEFT, OWN):
            span = chip_of(places[place])
            part = (
                partial_buf[place]
                + dot(key_w[0, span, :], slice_parts[:HEAD_DIM])
                + dot(key_w[1, span, :], slice_parts[HEAD_DIM:])
            )
            sums_stage[1, place] = part.astype(BF16).reshape(2, width, rows)
            sums[1]["mate", place].start()
    with jax.named_scope("sums1_first"):
        sums_first(1)
    with jax.named_scope("sums1_second"):
        sums_second(1)
    with jax.named_scope("sums0_last"):
        attention_ref[...] = sums_last(0).astype(BF16)
    with jax.named_scope("sums1_third"):
        sums_third(1)
    with jax.named_scope("inner_wait"):
        for step in range(1, tensor_size):
            inner_sends[step].wait_recv()
            inner_row = inner_row + inner_in[step, 0:1, :]
    inner_mean = inner_row / total_width
    unit_rows = rows_buf[0, shard_of(me), :].astype(F32) * factor_row
    with jax.named_scope("sums1_last"):
        shift = unit_rows * inner_mean
        grad_ref[...] = (factor_row * (gain_buf[shard_of(me), :] * sums_last(1) - shift)).astype(BF16)

    with jax.named_scope("drain"):
        for copies in (*gathers, *sums, memory_copies, mate_copies, back_copies, inner_sends):
            for copy in copies.values():
                copy.wait_send()


def finish(attention_in, grad_in, attention_ref, grad_ref):
    attention_ref[...] = attention_in[...]
    grad_ref[...] = grad_in[...]


def solution(mesh):
    seq_size, tensor_size = mesh.shape["seq"], mesh.shape["tensor"]

    def local(
        inputs,
        cotangent,
        norm_gain,
        head_gain,
        query_weight,
        key_weight,
        output_weight,
        modality,
        segments,
        block_order,
    ):
        rows, width = inputs.shape
        total_width = width * tensor_size
        heads = query_weight.shape[2] // HEAD_DIM
        vmem = pl.BlockSpec(memory_space=pltpu.VMEM)
        anywhere = pl.BlockSpec(memory_space=pl.ANY)
        dma = pltpu.SemaphoreType.DMA
        shape = jax.ShapeDtypeStruct((width, rows), BF16)
        block = (seq_size, rows, HEAD_DIM)
        attention_out, grad_input = pl.pallas_call(
            functools.partial(kernel, seq_size, tensor_size),
            out_shape=(shape, shape),
            in_specs=[anywhere] * 10,
            out_specs=(vmem, vmem),
            scratch_shapes=[
                pltpu.SMEM(block_order.shape, jnp.int32),
                pltpu.VMEM((1, rows), jnp.int32),
                pltpu.VMEM((seq_size, rows), jnp.int32),
                pltpu.VMEM(norm_gain.shape, F32),
                pltpu.VMEM(head_gain.shape, F32),
                pltpu.VMEM(query_weight.shape, BF16),
                pltpu.VMEM(key_weight.shape, BF16),
                pltpu.VMEM(output_weight.shape, BF16),
                pltpu.VMEM((2, total_width, rows), BF16),
                pltpu.VMEM((total_width, rows), F32),
                pltpu.VMEM((2, rows, heads * HEAD_DIM), F32),
                pltpu.VMEM((2, rows, HEAD_DIM), F32),
                pltpu.VMEM((2, heads * HEAD_DIM, rows), F32),
                pltpu.VMEM((heads * rows, HEAD_DIM), F32),
                pltpu.VMEM((rows, HEAD_DIM), F32),
                pltpu.VMEM((2, *block), BF16),
                pltpu.VMEM((heads * rows, HEAD_DIM), BF16),
                pltpu.VMEM((2, 4, 2, width, rows), BF16),
                pltpu.VMEM((2, 4, width, rows), BF16),
                pltpu.VMEM((2, 2, width // 2, rows), BF16),
                pltpu.VMEM((2, 3, width, rows), BF16),
                pltpu.VMEM((2, 2, width, rows), BF16),
                pltpu.VMEM((2, *block), BF16),
                pltpu.VMEM(block, BF16),
                pltpu.VMEM(block, BF16),
                pltpu.VMEM(block, BF16),
                pltpu.VMEM((4, 2 * width, rows), F32),
                pltpu.VMEM((8, rows), F32),
                pltpu.VMEM((tensor_size, 8, rows), F32),
                dma((10,)),
                dma((2, 14)),
                dma((2, 14)),
                dma((2 * seq_size,)),
                dma((2 * seq_size,)),
                dma((2, 10)),
                dma((2, 10)),
                dma((seq_size,)),
                dma((seq_size,)),
                dma((seq_size,)),
                dma((seq_size,)),
                dma((tensor_size,)),
                dma((tensor_size,)),
            ],
            compiler_params=pltpu.CompilerParams(collective_id=0, has_side_effects=True),
        )(
            block_order,
            modality.reshape(1, rows),
            segments.reshape(seq_size, rows),
            norm_gain,
            head_gain,
            inputs.T,
            cotangent.T,
            query_weight,
            key_weight,
            output_weight,
        )
        attention_out, grad_input = pl.pallas_call(
            finish, out_shape=(shape, shape), in_specs=[vmem, vmem], out_specs=(vmem, vmem)
        )(attention_out, grad_input)
        return attention_out.T, grad_input.T

    return jax.shard_map(
        local,
        mesh=mesh,
        in_specs=(
            P(("dp", "seq"), "tensor"),
            P(("dp", "seq"), "tensor"),
            P(),
            P(),
            P(None, None, "tensor"),
            P(None, None, "tensor"),
            P(None, "tensor", None),
            P(("dp", "seq")),
            P("dp"),
            P("dp"),
        ),
        out_specs=(P(("dp", "seq"), "tensor"), P(("dp", "seq"), "tensor")),
        check_vma=False,
    )
```

```python
import functools
import math

import jax
import jax.numpy as jnp
from jax import lax
from jax.experimental import pallas as pl
from jax.experimental.pallas import tpu as pltpu
from jax.sharding import PartitionSpec as P

HEAD_DIM = 128
EPSILON = 1e-06
MESH = pl.DeviceIdType.MESH
F32 = jnp.float32
BF16 = jnp.bfloat16

FAR, RIGHT, LEFT, OWN = range(4)


def dot(a, b):
    return jnp.dot(a, b, preferred_element_type=F32)


def dot_nt(a, b):
    return lax.dot_general(a, b, (((1,), (1,)), ((), ())), preferred_element_type=F32)


def dot_tn(a, b):
    return lax.dot_general(a, b, (((0,), (0,)), ((), ())), preferred_element_type=F32)


def remote(src, dst, send_sem, recv_sem, **device):
    return pltpu.make_async_remote_copy(
        src_ref=src,
        dst_ref=dst,
        send_sem=send_sem,
        recv_sem=recv_sem,
        device_id=device,
        device_id_type=MESH,
    )


def kernel(
    seq_size,
    tensor_size,
    order_hbm,
    modality_hbm,
    segments_hbm,
    norm_gain_hbm,
    head_gain_hbm,
    inputs_ref,
    cotangent_ref,
    query_hbm,
    key_hbm,
    output_hbm,
    attention_ref,
    grad_ref,
    order_ref,
    modality_ref,
    segments_ref,
    norm_gain_ref,
    head_gain_ref,
    query_w,
    key_w,
    output_w,
    rows_buf,
    gain_buf,
    query_acc,
    key_acc,
    back_acc,
    query_raw_buf,
    key_raw_buf,
    memory_buf,
    back_buf,
    sums_stage,
    sums_mate,
    sums_hop,
    sums_out,
    sums_final,
    memory_back,
    memory_mate,
    memory_out,
    memory_in,
    partial_buf,
    inner_out,
    inner_in,
    local_sem,
    gather_send,
    gather_recv,
    memory_send,
    memory_recv,
    sums_send,
    sums_recv,
    mate_send,
    mate_recv,
    back_send,
    back_recv,
    inner_send,
    inner_recv,
):
    seq = lax.axis_index("seq")
    me = lax.axis_index("tensor")
    core = lax.rem(me, 2)
    mate = me + 1 - 2 * core
    right = lax.rem(me + 2, tensor_size)
    left = lax.rem(me + tensor_size - 2, tensor_size)
    far = lax.rem(me + 4, tensor_size)
    width, rows = inputs_ref.shape
    half = width // 2
    total_width = width * tensor_size
    scale = 1.0 / math.sqrt(HEAD_DIM)
    quarter = half // 2
    quarters = [pl.ds(q * quarter, quarter) for q in range(4)]
    halves = [pl.ds(0, half), pl.ds(half, half)]

    pair = seq + 1 - 2 * lax.rem(seq, 2)
    turns = sorted(range(2, seq_size, 2), key=lambda step: -min(step, seq_size - step))
    greeted = [{"tensor": mate}, {"tensor": right}, {"tensor": left}, {"seq": pair}]
    greeted += [{"seq": lax.rem(seq + turn, seq_size)} for turn in turns]
    barrier = pltpu.get_barrier_semaphore()
    for device in greeted:
        pl.semaphore_signal(barrier, inc=1, device_id=device, device_id_type=MESH)

    def shard_of(slot, start=0, size=width):
        return pl.ds(pl.multiple_of(slot * width + start, 16), size)

    def chip_of(slot):
        return pl.ds(pl.multiple_of((slot - core) * width, 2 * width), 2 * width)

    loads = [
        pltpu.make_async_copy(src, dst, local_sem.at[k])
        for k, (src, dst) in enumerate(
            (
                (modality_hbm, modality_ref),
                (norm_gain_hbm, norm_gain_ref),
                (head_gain_hbm, head_gain_ref),
                (segments_hbm, segments_ref),
                (order_hbm, order_ref),
                (inputs_ref, rows_buf.at[0, shard_of(me)]),
                (query_hbm, query_w),
                (key_hbm, key_w),
                (output_hbm, output_w),
                (cotangent_ref, rows_buf.at[1, shard_of(me)]),
            )
        )
    ]
    for copy in loads:
        copy.start()
    pl.semaphore_wait(barrier, len(greeted))

    def gather(k):
        own = (inputs_ref, cotangent_ref)[k]
        copies = {}

        def add(name, which, device, start=0, size=width, from_input=False):
            there = rows_buf.at[k, shard_of(which, start, size)]
            here = own.at[pl.ds(start, size)] if from_input else there
            index = len(copies)
            copies[name] = remote(here, there, gather_send.at[k, index], gather_recv.at[k, index], tensor=device)

        add(("mate", OWN), me, mate, from_input=True)
        for q in range(4):
            add((RIGHT, q), me, right, q * quarter, quarter, True)
            add((LEFT, q), me, left, q * quarter, quarter, True)
            add((FAR, q), left if q < 2 else right, right if q < 2 else left, q * quarter, quarter)
            add(("mate", FAR, q), far, mate, q * quarter, quarter)
        for h in range(2):
            add(("mate", LEFT, h), left, mate, h * half, half)
            add(("mate", RIGHT, h), right, mate, h * half, half)
        return copies

    gathers = [gather(0), gather(1)]

    def gather_start(k):
        for q in range(2):
            gathers[k][RIGHT, q].start()
            gathers[k][LEFT, q + 2].start()
        gathers[k]["mate", OWN].start()
        for q in range(2):
            gathers[k][RIGHT, q + 2].start()
            gathers[k][LEFT, q].start()

    def gather_first(k):
        copies = gathers[k]
        for q in range(2):
            copies[RIGHT, q].wait_recv()
            copies[FAR, q].start()
            copies[LEFT, q + 2].wait_recv()
            copies[FAR, q + 2].start()
        copies["mate", LEFT, 0].start()
        copies["mate", RIGHT, 1].start()

    def gather_near(k):
        copies = gathers[k]
        for q in range(2):
            copies[RIGHT, q + 2].wait_recv()
        copies["mate", LEFT, 1].start()
        for q in range(2):
            copies[LEFT, q].wait_recv()
        copies["mate", RIGHT, 0].start()

    def gather_far(k):
        copies = gathers[k]
        for q in (0, 2, 1, 3):
            copies[FAR, q].wait_recv()
            copies["mate", FAR, q].start()

    def from_mate(k, place):
        copies = gathers[k]
        if place == OWN:
            copies["mate", OWN].wait_recv()
        else:
            for piece in range(4 if place == FAR else 2):
                copies["mate", place, piece].wait_recv()

    gather_start(0)

    row_of = lax.broadcasted_iota(jnp.int32, (rows, rows), 0)
    col_of = lax.broadcasted_iota(jnp.int32, (rows, rows), 1)
    diagonal = row_of == col_of

    def as_column(row):
        return jnp.sum(jnp.where(diagonal, row, 0.0), axis=1, keepdims=True)

    def as_row(column):
        return jnp.sum(jnp.where(diagonal, column, 0.0), axis=0, keepdims=True)

    for copy in loads[:5]:
        copy.wait()
    image_row = (modality_ref[...] == 1).astype(F32)
    is_image = as_column(image_row) > 0.5
    image_pick = jnp.broadcast_to(is_image, (rows, HEAD_DIM))
    image_pick_t = jnp.broadcast_to(image_row > 0.5, (HEAD_DIM, rows))
    for k in range(total_width // HEAD_DIM):
        columns = slice(k * HEAD_DIM, (k + 1) * HEAD_DIM)
        gain_buf[columns, :] = jnp.where(image_pick, norm_gain_ref[1:2, columns], norm_gain_ref[0:1, columns]).T

    def segments_of(block):
        return segments_ref[pl.ds(order_ref[block], 1), :].astype(F32)

    heads = query_acc.shape[2] // HEAD_DIM
    depth = heads * HEAD_DIM
    key_segments = jnp.concatenate([segments_of(k) for k in range(seq_size)], axis=1)
    query_segments = jnp.concatenate([as_column(segments_of(seq))] * heads, axis=0)
    query_acc[...] = jnp.zeros_like(query_acc)
    key_acc[...] = jnp.zeros_like(key_acc)
    back_acc[...] = jnp.zeros_like(back_acc)

    def scaled_rows(slot):
        span = chip_of(slot)
        x = rows_buf[0, span, :].astype(F32)
        return (x * gain_buf[span, :]).T.astype(BF16), jnp.sum(x * x, axis=0, keepdims=True)

    def project_key(slot, scaled):
        for e in range(2):
            key_acc[e] += dot(scaled, key_w[e, chip_of(slot), :])

    def project_query(slot, scaled):
        for e in range(2):
            query_acc[e] += dot(scaled, query_w[e, chip_of(slot), :])

    def project(slot, squares):
        scaled, more = scaled_rows(slot)
        project_key(slot, scaled)
        project_query(slot, scaled)
        return squares + more

    squares = jnp.zeros((1, rows), F32)
    gather_first(0)
    gather_start(1)
    for copy in loads[5:8]:
        copy.wait()
    from_mate(0, OWN)
    squares = project(me, squares)
    gather_near(0)
    from_mate(0, LEFT)
    squares = project(left, squares)
    from_mate(0, RIGHT)
    squares = project(right, squares)
    gather_far(0)
    from_mate(0, FAR)
    far_scaled, more = scaled_rows(far)
    squares = squares + more
    project_key(far, far_scaled)

    factor_row = lax.rsqrt(squares / total_width + EPSILON)
    row_factor = as_column(factor_row)

    def picked(acc, columns):
        return jnp.where(image_pick, acc[1, :, columns], acc[0, :, columns]) * row_factor

    def head_factor(raw):
        return lax.rsqrt(jnp.mean(raw * raw, axis=-1, keepdims=True) + EPSILON)

    def head_gain(kind):
        return jnp.where(image_pick, head_gain_ref[1, kind : kind + 1, :], head_gain_ref[0, kind : kind + 1, :])

    key_raw = picked(key_acc, slice(None))
    key_raw_buf[...] = key_raw
    key_normed = key_raw * head_factor(key_raw) * head_gain(1)
    memory_buf[core, seq] = jnp.where(core == 0, key_normed, key_raw).astype(BF16)

    memory_copies = {}

    def memory_add(name, block, device):
        index = len(memory_copies)
        ref = memory_buf.at[core, block]
        memory_copies[name] = remote(ref, ref, memory_send.at[index], memory_recv.at[index], **device)

    memory_add("pair", seq, {"seq": pair})
    arrivals = [(seq, None, ("mate", "own", 0)), (pair, ("pair"), ("mate", "pair", 0))]
    for name, block in (("own", seq), ("pair", pair)):
        memory_add(("mate", name, 0), block, {"tensor": mate})
        for turn in turns:
            memory_add((name, turn), block, {"seq": lax.rem(seq + turn, seq_size)})
            behind = lax.rem(block + seq_size - turn, seq_size)
            memory_add(("mate", name, turn), behind, {"tensor": mate})
            arrivals.append((behind, (name, turn), ("mate", name, turn)))
    arrivals = arrivals[:1] + arrivals[2 : 2 + len(turns)] + arrivals[1:2] + arrivals[2 + len(turns) :]

    memory_copies["pair"].start()
    for turn in turns:
        memory_copies["own", turn].start()
    memory_copies["mate", "own", 0].start()

    project_query(far, far_scaled)
    gather_first(1)

    memory_copies["pair"].wait_recv()
    for turn in turns:
        memory_copies["pair", turn].start()
    memory_copies["mate", "pair", 0].start()

    for h in range(heads):
        raw = picked(query_acc, slice(h * HEAD_DIM, (h + 1) * HEAD_DIM))
        query_raw_buf[h * rows : (h + 1) * rows] = raw
    query_gain = jnp.concatenate([head_gain(0)] * heads, axis=0)
    query_raw = query_raw_buf[...]
    query_normed = (query_raw * head_factor(query_raw) * query_gain).astype(BF16)

    def back_project(slot):
        span = chip_of(slot)
        for e in range(2):
            back_acc[e] += dot(output_w[e, :, span], rows_buf[1, span, :])

    loads[8].wait()
    loads[9].wait()
    from_mate(1, OWN)
    back_project(me)

    for turn in turns:
        memory_copies["own", turn].wait_recv()
        memory_copies["mate", "own", turn].start()
    gather_near(1)
    from_mate(1, LEFT)
    back_project(left)
    gather_far(1)
    for turn in turns:
        memory_copies["pair", turn].wait_recv()
        memory_copies["mate", "pair", turn].start()
    from_mate(1, RIGHT)
    back_project(right)
    from_mate(1, FAR)
    back_project(far)
    head_rows = [slice(h * rows, (h + 1) * rows) for h in range(heads)]
    for h in range(heads):
        columns = slice(h * HEAD_DIM, (h + 1) * HEAD_DIM)
        back_buf[head_rows[h]] = jnp.where(
            image_pick_t, back_acc[1, columns, :], back_acc[0, columns, :]
        ).T.astype(BF16)
    back_attended = back_buf[...]
    for _, _, handed in arrivals:
        memory_copies[handed].wait_recv()

    all_rows = seq_size * rows
    keys = memory_buf[0].reshape(all_rows, HEAD_DIM)
    values = memory_buf[1].reshape(all_rows, HEAD_DIM)
    scores = dot_nt(query_normed, keys) * scale
    weights = jnp.where(key_segments <= query_segments, jnp.exp(scores), 0.0).astype(BF16)
    denominator = jnp.sum(weights.astype(F32), axis=1, keepdims=True)
    attended = (dot(weights, values) / denominator).astype(BF16)
    places = {FAR: far, RIGHT: right, LEFT: left, OWN: me}

    def by_expert(parts, picks, axis):
        zero = jnp.zeros_like(parts)
        return jnp.concatenate(
            [jnp.where(picks, zero, parts), jnp.where(picks, parts, zero)], axis=axis
        ).astype(BF16)

    def sums_copies(k):
        copies = {}

        def add(name, src, dst, device):
            index = len(copies)
            copies[name] = remote(src, dst, sums_send.at[k, index], sums_recv.at[k, index], tensor=device)

        for place in range(4):
            add(("mate", place), sums_stage.at[k, place, 1 - core], sums_mate.at[k, place], mate)
        for q, part in enumerate(quarters):
            device, place, side = (right, RIGHT, 0) if q < 2 else (left, LEFT, 1)
            add((FAR, q), sums_out.at[k, FAR, part], sums_hop.at[k, q], device)
            add((place, q), sums_out.at[k, place, part], sums_final.at[k, side, part], device)
        for place, side, device, part in ((RIGHT, 0, right, halves[1]), (LEFT, 1, left, halves[0])):
            add((place, "half"), sums_out.at[k, place, part], sums_final.at[k, side, part], device)
        return copies

    sums = [sums_copies(0), sums_copies(1)]

    def chip_sum(k, place, part=slice(None)):
        return sums_stage[k, place, core, part].astype(F32) + sums_mate[k, place, part].astype(F32)

    def sums_first(k):
        sums[k]["mate", FAR].wait_recv()
        for q in (0, 2, 1, 3):
            sums_out[k, FAR, quarters[q]] = chip_sum(k, FAR, quarters[q]).astype(BF16)
            sums[k][FAR, q].start()

    def sums_second(k):
        for place, part in ((RIGHT, halves[1]), (LEFT, halves[0])):
            sums[k]["mate", place].wait_recv()
            sums_out[k, place, part] = chip_sum(k, place, part).astype(BF16)
            sums[k][place, "half"].start()

    def sums_third(k):
        for q in (0, 2, 1, 3):
            place, part = RIGHT if q < 2 else LEFT, quarters[q]
            sums[k][FAR, q].wait_recv()
            sums_out[k, place, part] = (chip_sum(k, place, part) + sums_hop[k, q].astype(F32)).astype(BF16)
            sums[k][place, q].start()

    def sums_last(k, write):
        sums[k]["mate", OWN].wait_recv()
        sums[k][RIGHT, "half"].wait_recv()
        sums[k][LEFT, "half"].wait_recv()
        for q in (0, 2, 1, 3):
            part = quarters[q]
            sums[k][RIGHT if q < 2 else LEFT, q].wait_recv()
            write(
                q,
                chip_sum(k, OWN, part)
                + sums_final[k, 0, part].astype(F32)
                + sums_final[k, 1, part].astype(F32),
            )

    def side_by_side(stacked):
        return jnp.concatenate([stacked[r] for r in head_rows], axis=1)

    wide_pick = jnp.broadcast_to(is_image, (rows, depth))
    attended_parts = by_expert(side_by_side(attended.astype(F32)), wide_pick, 1)

    def out_project(place):
        span = chip_of(places[place])
        block = dot(attended_parts[:, :depth], output_w[0, :, span]) + dot(
            attended_parts[:, depth:], output_w[1, :, span]
        )
        sums_stage[0, place] = block.T.astype(BF16).reshape(2, width, rows)
        sums[0]["mate", place].start()

    out_project(FAR)
    offset = jnp.sum(back_attended.astype(F32) * attended.astype(F32), axis=1, keepdims=True)

    outgoing = [("pair", turn, lax.rem(pair + turn, seq_size)) for turn in turns]
    outgoing += [("own", turn, lax.rem(seq + turn, seq_size)) for turn in turns]
    outgoing += [("pair", 0, pair), ("own", 0, seq)]
    mate_copies, back_copies = {}, {}
    for index, (name, turn, block) in enumerate(outgoing):
        mate_copies[index] = remote(
            memory_back.at[1 - core, block],
            memory_mate.at[index],
            mate_send.at[index],
            mate_recv.at[index],
            tensor=mate,
        )
        target = lax.rem(seq + turn, seq_size)
        if turn > 0 or name == "pair":
            back_copies[name, turn] = remote(
                memory_out.at[index],
                memory_in.at[index],
                back_send.at[index],
                back_recv.at[index],
                seq=target if turn > 0 else pair,
            )
    in_slot = {(name, turn): index for index, (name, turn, _) in enumerate(outgoing)}
    probability = (weights.astype(F32) / denominator).astype(BF16)
    back_probability = dot_nt(back_attended, values)
    back_score = (probability.astype(F32) * (back_probability - offset)).astype(BF16)
    memory_back[0] = (dot_tn(back_score, query_normed) * scale).astype(BF16).reshape(seq_size, rows, HEAD_DIM)
    memory_back[1] = dot_tn(probability, back_attended).astype(BF16).reshape(seq_size, rows, HEAD_DIM)
    for copy in mate_copies.values():
        copy.start()

    sums_first(0)
    out_project(RIGHT)

    kept = {}
    for index, (name, turn, block) in enumerate(outgoing):
        mate_copies[index].wait_recv()
        both = memory_back[core, block].astype(F32) + memory_mate[index].astype(F32)
        if turn > 0:
            memory_out[index] = both.astype(BF16)
            back_copies[name, turn].start()
        else:
            kept[name] = both

    out_project(LEFT)
    out_project(OWN)
    sums_second(0)

    back_query = dot(back_score, keys)
    query_factor = head_factor(query_raw)
    query_unit = query_raw * query_factor
    weighted = query_gain * (back_query * scale)
    query_back = query_factor * (
        weighted - query_unit * jnp.mean(weighted * query_unit, axis=-1, keepdims=True)
    )
    query_back = query_back.astype(BF16).astype(F32)
    inner = jnp.sum(side_by_side(query_back * query_raw), axis=1, keepdims=True)
    back_columns = jnp.concatenate([query_back[r].T for r in head_rows], axis=0)
    query_parts = by_expert(back_columns, jnp.concatenate([image_pick_t] * heads, axis=0), 0)
    for place in (FAR, RIGHT, LEFT, OWN):
        span = chip_of(places[place])
        partial_buf[place] = dot(query_w[0, span, :], query_parts[:depth]) + dot(
            query_w[1, span, :], query_parts[depth:]
        )

    def received(name):
        total = kept[name]
        for turn in turns:
            back_copies[name, turn].wait_recv()
            total = total + memory_in[in_slot[name, turn]].astype(F32)
        return total

    memory_out[in_slot["pair", 0]] = received("pair").astype(BF16)
    back_copies["pair", 0].start()
    sums_third(0)
    slice_grad = received("own")
    back_copies["pair", 0].wait_recv()
    slice_grad = slice_grad + memory_in[in_slot["pair", 0]].astype(F32)
    key_raw = key_raw_buf[...]
    key_factor = head_factor(key_raw)
    key_unit = key_raw * key_factor
    weighted = head_gain(1) * slice_grad
    key_back = key_factor * (weighted - key_unit * jnp.mean(weighted * key_unit, axis=-1, keepdims=True))
    slice_back = jnp.where(core == 0, key_back, slice_grad).astype(BF16).astype(F32)
    slice_parts = by_expert(slice_back.T, image_pick_t, 0)

    inner = inner + jnp.sum(slice_back * key_raw, axis=1, keepdims=True)
    inner_row = as_row(inner)
    inner_out[...] = jnp.broadcast_to(inner_row, inner_out.shape)
    inner_sends = {}
    for step in range(1, tensor_size):
        inner_sends[step] = remote(
            inner_out,
            inner_in.at[step],
            inner_send.at[step],
            inner_recv.at[step],
            tensor=lax.rem(me + step, tensor_size),
        )
        inner_sends[step].start()

    def key_project(place, parity):
        slot = places[place] - core + parity
        part = pl.ds(pl.multiple_of(parity * width, 64), width)
        total = (
            partial_buf[place, part, :]
            + dot(key_w[0, shard_of(slot), :], slice_parts[:HEAD_DIM])
            + dot(key_w[1, shard_of(slot), :], slice_parts[HEAD_DIM:])
        )
        sums_stage[1, place, parity] = total.astype(BF16)

    for place in (FAR, RIGHT, LEFT):
        key_project(place, 1 - core)
        sums[1]["mate", place].start()
        if place == FAR:
            key_project(place, core)
    key_project(OWN, 1 - core)
    sums[1]["mate", OWN].start()
    sums_first(1)
    key_project(RIGHT, core)
    key_project(LEFT, core)
    sums_second(1)
    key_project(OWN, core)

    def write_attention(q, total):
        attention_ref[quarters[q], :] = total.astype(BF16)

    sums_last(0, write_attention)
    sums_third(1)
    for step in range(1, tensor_size):
        inner_sends[step].wait_recv()
        inner_row = inner_row + inner_in[step, 0:1, :]
    inner_mean = inner_row / total_width

    def write_grad(q, total):
        here = shard_of(me, q * quarter, quarter)
        shift = rows_buf[0, here, :].astype(F32) * (factor_row * inner_mean)
        grad_ref[quarters[q], :] = (factor_row * (gain_buf[here, :] * total - shift)).astype(BF16)

    sums_last(1, write_grad)

    for copies in (*gathers, *sums, memory_copies, mate_copies, back_copies, inner_sends):
        for copy in copies.values():
            copy.wait_send()


def finish(attention_in, grad_in, attention_ref, grad_ref):
    attention_ref[...] = attention_in[...]
    grad_ref[...] = grad_in[...]


def solution(mesh):
    seq_size, tensor_size = mesh.shape["seq"], mesh.shape["tensor"]

    def local(
        inputs,
        cotangent,
        norm_gain,
        head_gain,
        query_weight,
        key_weight,
        output_weight,
        modality,
        segments,
        block_order,
    ):
        rows, width = inputs.shape
        total_width = width * tensor_size
        heads = query_weight.shape[2] // HEAD_DIM
        vmem = pl.BlockSpec(memory_space=pltpu.VMEM)
        anywhere = pl.BlockSpec(memory_space=pl.ANY)
        dma = pltpu.SemaphoreType.DMA
        shape = jax.ShapeDtypeStruct((width, rows), BF16)
        block = (seq_size, rows, HEAD_DIM)
        attention_out, grad_input = pl.pallas_call(
            functools.partial(kernel, seq_size, tensor_size),
            out_shape=(shape, shape),
            in_specs=[anywhere] * 10,
            out_specs=(vmem, vmem),
            scratch_shapes=[
                pltpu.SMEM(block_order.shape, jnp.int32),
                pltpu.VMEM((1, rows), jnp.int32),
                pltpu.VMEM((seq_size, rows), jnp.int32),
                pltpu.VMEM(norm_gain.shape, F32),
                pltpu.VMEM(head_gain.shape, F32),
                pltpu.VMEM(query_weight.shape, BF16),
                pltpu.VMEM(key_weight.shape, BF16),
                pltpu.VMEM(output_weight.shape, BF16),
                pltpu.VMEM((2, total_width, rows), BF16),
                pltpu.VMEM((total_width, rows), F32),
                pltpu.VMEM((2, rows, heads * HEAD_DIM), F32),
                pltpu.VMEM((2, rows, HEAD_DIM), F32),
                pltpu.VMEM((2, heads * HEAD_DIM, rows), F32),
                pltpu.VMEM((heads * rows, HEAD_DIM), F32),
                pltpu.VMEM((rows, HEAD_DIM), F32),
                pltpu.VMEM((2, *block), BF16),
                pltpu.VMEM((heads * rows, HEAD_DIM), BF16),
                pltpu.VMEM((2, 4, 2, width, rows), BF16),
                pltpu.VMEM((2, 4, width, rows), BF16),
                pltpu.VMEM((2, 4, width // 4, rows), BF16),
                pltpu.VMEM((2, 3, width, rows), BF16),
                pltpu.VMEM((2, 2, width, rows), BF16),
                pltpu.VMEM((2, *block), BF16),
                pltpu.VMEM(block, BF16),
                pltpu.VMEM(block, BF16),
                pltpu.VMEM(block, BF16),
                pltpu.VMEM((4, 2 * width, rows), F32),
                pltpu.VMEM((8, rows), F32),
                pltpu.VMEM((tensor_size, 8, rows), F32),
                dma((10,)),
                dma((2, 21)),
                dma((2, 21)),
                dma((2 * seq_size,)),
                dma((2 * seq_size,)),
                dma((2, 14)),
                dma((2, 14)),
                dma((seq_size,)),
                dma((seq_size,)),
                dma((seq_size,)),
                dma((seq_size,)),
                dma((tensor_size,)),
                dma((tensor_size,)),
            ],
            compiler_params=pltpu.CompilerParams(collective_id=0, has_side_effects=True),
        )(
            block_order,
            modality.reshape(1, rows),
            segments.reshape(seq_size, rows),
            norm_gain,
            head_gain,
            inputs.T,
            cotangent.T,
            query_weight,
            key_weight,
            output_weight,
        )
        attention_out, grad_input = pl.pallas_call(
            finish, out_shape=(shape, shape), in_specs=[vmem, vmem], out_specs=(vmem, vmem)
        )(attention_out, grad_input)
        return attention_out.T, grad_input.T

    return jax.shard_map(
        local,
        mesh=mesh,
        in_specs=(
            P(("dp", "seq"), "tensor"),
            P(("dp", "seq"), "tensor"),
            P(),
            P(),
            P(None, None, "tensor"),
            P(None, None, "tensor"),
            P(None, "tensor", None),
            P(("dp", "seq")),
            P("dp"),
            P("dp"),
        ),
        out_specs=(P(("dp", "seq"), "tensor"), P(("dp", "seq"), "tensor")),
        check_vma=False,
    )
```

```python
import functools
import math

import jax
import jax.numpy as jnp
from jax import lax
from jax.experimental import pallas as pl
from jax.experimental.pallas import tpu as pltpu
from jax.sharding import PartitionSpec as P

HEAD_DIM = 128
EPSILON = 1e-06
MESH = pl.DeviceIdType.MESH
F32 = jnp.float32
BF16 = jnp.bfloat16

FAR, RIGHT, LEFT, OWN = range(4)


def dot(a, b):
    return jnp.dot(a, b, preferred_element_type=F32)


def dot_nt(a, b):
    return lax.dot_general(a, b, (((1,), (1,)), ((), ())), preferred_element_type=F32)


def dot_tn(a, b):
    return lax.dot_general(a, b, (((0,), (0,)), ((), ())), preferred_element_type=F32)


def remote(src, dst, send_sem, recv_sem, **device):
    return pltpu.make_async_remote_copy(
        src_ref=src,
        dst_ref=dst,
        send_sem=send_sem,
        recv_sem=recv_sem,
        device_id=device,
        device_id_type=MESH,
    )


def kernel(
    seq_size,
    tensor_size,
    order_hbm,
    modality_hbm,
    segments_hbm,
    norm_gain_hbm,
    head_gain_hbm,
    inputs_ref,
    cotangent_ref,
    query_hbm,
    key_hbm,
    output_hbm,
    attention_ref,
    grad_ref,
    order_ref,
    modality_ref,
    segments_ref,
    norm_gain_ref,
    head_gain_ref,
    query_w,
    key_w,
    output_w,
    rows_buf,
    gain_buf,
    query_acc,
    key_acc,
    back_acc,
    query_raw_buf,
    key_raw_buf,
    memory_buf,
    back_buf,
    sums_stage,
    sums_mate,
    sums_hop,
    sums_out,
    sums_final,
    memory_back,
    memory_mate,
    memory_out,
    memory_in,
    partial_buf,
    inner_out,
    inner_in,
    local_sem,
    gather_send,
    gather_recv,
    memory_send,
    memory_recv,
    sums_send,
    sums_recv,
    mate_send,
    mate_recv,
    back_send,
    back_recv,
    inner_send,
    inner_recv,
):
    seq = lax.axis_index("seq")
    me = lax.axis_index("tensor")
    core = lax.rem(me, 2)
    mate = me + 1 - 2 * core
    right = lax.rem(me + 2, tensor_size)
    left = lax.rem(me + tensor_size - 2, tensor_size)
    far = lax.rem(me + 4, tensor_size)
    width, rows = inputs_ref.shape
    half = width // 2
    total_width = width * tensor_size
    scale = 1.0 / math.sqrt(HEAD_DIM)
    quarter = half // 2
    quarters = [pl.ds(q * quarter, quarter) for q in range(4)]
    halves = [pl.ds(0, half), pl.ds(half, half)]

    pair = seq + 1 - 2 * lax.rem(seq, 2)
    turns = sorted(range(2, seq_size, 2), key=lambda step: -min(step, seq_size - step))
    greeted = [{"tensor": mate}, {"tensor": right}, {"tensor": left}, {"seq": pair}]
    greeted += [{"seq": lax.rem(seq + turn, seq_size)} for turn in turns]
    barrier = pltpu.get_barrier_semaphore()
    for device in greeted:
        pl.semaphore_signal(barrier, inc=1, device_id=device, device_id_type=MESH)

    def shard_of(slot, start=0, size=width):
        return pl.ds(pl.multiple_of(slot * width + start, 16), size)

    def chip_of(slot):
        return pl.ds(pl.multiple_of((slot - core) * width, 2 * width), 2 * width)

    loads = [
        pltpu.make_async_copy(src, dst, local_sem.at[k])
        for k, (src, dst) in enumerate(
            (
                (modality_hbm, modality_ref),
                (norm_gain_hbm, norm_gain_ref),
                (head_gain_hbm, head_gain_ref),
                (segments_hbm, segments_ref),
                (order_hbm, order_ref),
                (inputs_ref, rows_buf.at[0, shard_of(me)]),
                (query_hbm, query_w),
                (key_hbm, key_w),
                (output_hbm, output_w),
                (cotangent_ref, rows_buf.at[1, shard_of(me)]),
            )
        )
    ]
    for copy in loads:
        copy.start()
    pl.semaphore_wait(barrier, len(greeted))

    def gather(k):
        own = (inputs_ref, cotangent_ref)[k]
        copies = {}

        def add(name, which, device, start=0, size=width, from_input=False):
            there = rows_buf.at[k, shard_of(which, start, size)]
            here = own.at[pl.ds(start, size)] if from_input else there
            index = len(copies)
            copies[name] = remote(here, there, gather_send.at[k, index], gather_recv.at[k, index], tensor=device)

        add(("mate", OWN), me, mate, from_input=True)
        for q in range(4):
            add((RIGHT, q), me, right, q * quarter, quarter, True)
            add((LEFT, q), me, left, q * quarter, quarter, True)
            add((FAR, q), left if q < 2 else right, right if q < 2 else left, q * quarter, quarter)
            add(("mate", FAR, q), far, mate, q * quarter, quarter)
        for h in range(2):
            add(("mate", LEFT, h), left, mate, h * half, half)
            add(("mate", RIGHT, h), right, mate, h * half, half)
        return copies

    gathers = [gather(0), gather(1)]

    def gather_start(k):
        for q in range(2):
            gathers[k][RIGHT, q].start()
            gathers[k][LEFT, q + 2].start()
        gathers[k]["mate", OWN].start()
        for q in range(2):
            gathers[k][RIGHT, q + 2].start()
            gathers[k][LEFT, q].start()

    def gather_first(k):
        copies = gathers[k]
        for q in range(2):
            copies[RIGHT, q].wait_recv()
            copies[FAR, q].start()
            copies[LEFT, q + 2].wait_recv()
            copies[FAR, q + 2].start()
        copies["mate", LEFT, 0].start()
        copies["mate", RIGHT, 1].start()

    def gather_near(k):
        copies = gathers[k]
        for q in range(2):
            copies[RIGHT, q + 2].wait_recv()
        copies["mate", LEFT, 1].start()
        for q in range(2):
            copies[LEFT, q].wait_recv()
        copies["mate", RIGHT, 0].start()

    def gather_far(k):
        copies = gathers[k]
        for q in (0, 2, 1, 3):
            copies[FAR, q].wait_recv()
            copies["mate", FAR, q].start()

    def from_mate(k, place):
        copies = gathers[k]
        if place == OWN:
            copies["mate", OWN].wait_recv()
        else:
            for piece in range(4 if place == FAR else 2):
                copies["mate", place, piece].wait_recv()

    gather_start(0)

    row_of = lax.broadcasted_iota(jnp.int32, (rows, rows), 0)
    col_of = lax.broadcasted_iota(jnp.int32, (rows, rows), 1)
    diagonal = row_of == col_of

    def as_column(row):
        return jnp.sum(jnp.where(diagonal, row, 0.0), axis=1, keepdims=True)

    def as_row(column):
        return jnp.sum(jnp.where(diagonal, column, 0.0), axis=0, keepdims=True)

    for copy in loads[:5]:
        copy.wait()
    image_row = (modality_ref[...] == 1).astype(F32)
    is_image = as_column(image_row) > 0.5
    image_pick = jnp.broadcast_to(is_image, (rows, HEAD_DIM))
    image_pick_t = jnp.broadcast_to(image_row > 0.5, (HEAD_DIM, rows))
    for k in range(total_width // HEAD_DIM):
        columns = slice(k * HEAD_DIM, (k + 1) * HEAD_DIM)
        gain_buf[columns, :] = jnp.where(image_pick, norm_gain_ref[1:2, columns], norm_gain_ref[0:1, columns]).T

    def segments_of(block):
        return segments_ref[pl.ds(order_ref[block], 1), :].astype(F32)

    heads = query_acc.shape[2] // HEAD_DIM
    depth = heads * HEAD_DIM
    key_segments = jnp.concatenate([segments_of(k) for k in range(seq_size)], axis=1)
    query_segments = jnp.concatenate([as_column(segments_of(seq))] * heads, axis=0)
    query_acc[...] = jnp.zeros_like(query_acc)
    key_acc[...] = jnp.zeros_like(key_acc)
    back_acc[...] = jnp.zeros_like(back_acc)

    def scaled_rows(slot):
        span = chip_of(slot)
        x = rows_buf[0, span, :].astype(F32)
        return (x * gain_buf[span, :]).T.astype(BF16), jnp.sum(x * x, axis=0, keepdims=True)

    def project_key(slot, scaled):
        for e in range(2):
            key_acc[e] += dot(scaled, key_w[e, chip_of(slot), :])

    def project_query(slot, scaled):
        for e in range(2):
            query_acc[e] += dot(scaled, query_w[e, chip_of(slot), :])

    def project(slot, squares):
        scaled, more = scaled_rows(slot)
        project_key(slot, scaled)
        project_query(slot, scaled)
        return squares + more

    squares = jnp.zeros((1, rows), F32)
    gather_first(0)
    gather_start(1)
    for copy in loads[5:8]:
        copy.wait()
    from_mate(0, OWN)
    squares = project(me, squares)
    gather_near(0)
    from_mate(0, LEFT)
    squares = project(left, squares)
    from_mate(0, RIGHT)
    squares = project(right, squares)
    gather_far(0)
    from_mate(0, FAR)
    far_scaled, more = scaled_rows(far)
    squares = squares + more
    project_key(far, far_scaled)

    factor_row = lax.rsqrt(squares / total_width + EPSILON)
    row_factor = as_column(factor_row)

    def picked(acc, columns):
        return jnp.where(image_pick, acc[1, :, columns], acc[0, :, columns]) * row_factor

    def head_factor(raw):
        return lax.rsqrt(jnp.mean(raw * raw, axis=-1, keepdims=True) + EPSILON)

    def head_gain(kind):
        return jnp.where(image_pick, head_gain_ref[1, kind : kind + 1, :], head_gain_ref[0, kind : kind + 1, :])

    key_raw = picked(key_acc, slice(None))
    key_raw_buf[...] = key_raw
    key_normed = key_raw * head_factor(key_raw) * head_gain(1)
    memory_buf[core, seq] = jnp.where(core == 0, key_normed, key_raw).astype(BF16)

    memory_copies = {}

    def memory_add(name, block, device):
        index = len(memory_copies)
        ref = memory_buf.at[core, block]
        memory_copies[name] = remote(ref, ref, memory_send.at[index], memory_recv.at[index], **device)

    memory_add("pair", seq, {"seq": pair})
    arrivals = [(seq, None, ("mate", "own", 0)), (pair, ("pair"), ("mate", "pair", 0))]
    for name, block in (("own", seq), ("pair", pair)):
        memory_add(("mate", name, 0), block, {"tensor": mate})
        for turn in turns:
            memory_add((name, turn), block, {"seq": lax.rem(seq + turn, seq_size)})
            behind = lax.rem(block + seq_size - turn, seq_size)
            memory_add(("mate", name, turn), behind, {"tensor": mate})
            arrivals.append((behind, (name, turn), ("mate", name, turn)))
    arrivals = arrivals[:1] + arrivals[2 : 2 + len(turns)] + arrivals[1:2] + arrivals[2 + len(turns) :]

    memory_copies["pair"].start()
    for turn in turns:
        memory_copies["own", turn].start()
    memory_copies["mate", "own", 0].start()

    project_query(far, far_scaled)
    gather_first(1)

    memory_copies["pair"].wait_recv()
    for turn in turns:
        memory_copies["pair", turn].start()
    memory_copies["mate", "pair", 0].start()

    for h in range(heads):
        raw = picked(query_acc, slice(h * HEAD_DIM, (h + 1) * HEAD_DIM))
        query_raw_buf[h * rows : (h + 1) * rows] = raw
    query_gain = jnp.concatenate([head_gain(0)] * heads, axis=0)
    query_raw = query_raw_buf[...]
    query_normed = (query_raw * head_factor(query_raw) * query_gain).astype(BF16)

    def back_project(slot):
        span = chip_of(slot)
        for e in range(2):
            back_acc[e] += dot(output_w[e, :, span], rows_buf[1, span, :])

    loads[8].wait()
    loads[9].wait()
    from_mate(1, OWN)
    back_project(me)

    for turn in turns:
        memory_copies["own", turn].wait_recv()
        memory_copies["mate", "own", turn].start()
    gather_near(1)
    from_mate(1, LEFT)
    back_project(left)
    gather_far(1)
    for turn in turns:
        memory_copies["pair", turn].wait_recv()
        memory_copies["mate", "pair", turn].start()
    from_mate(1, RIGHT)
    back_project(right)
    from_mate(1, FAR)
    back_project(far)
    head_rows = [slice(h * rows, (h + 1) * rows) for h in range(heads)]
    for h in range(heads):
        columns = slice(h * HEAD_DIM, (h + 1) * HEAD_DIM)
        back_buf[head_rows[h]] = jnp.where(
            image_pick_t, back_acc[1, columns, :], back_acc[0, columns, :]
        ).T.astype(BF16)
    back_attended = back_buf[...]
    for _, _, handed in arrivals:
        memory_copies[handed].wait_recv()

    all_rows = seq_size * rows
    keys = memory_buf[0].reshape(all_rows, HEAD_DIM)
    values = memory_buf[1].reshape(all_rows, HEAD_DIM)
    scores = dot_nt(query_normed, keys) * scale
    weights = jnp.where(key_segments <= query_segments, jnp.exp(scores), 0.0).astype(BF16)
    denominator = jnp.sum(weights.astype(F32), axis=1, keepdims=True)
    attended = (dot(weights, values) / denominator).astype(BF16)
    places = {FAR: far, RIGHT: right, LEFT: left, OWN: me}

    def by_expert(parts, picks, axis):
        zero = jnp.zeros_like(parts)
        return jnp.concatenate(
            [jnp.where(picks, zero, parts), jnp.where(picks, parts, zero)], axis=axis
        ).astype(BF16)

    def sums_copies(k):
        copies = {}

        def add(name, src, dst, device):
            index = len(copies)
            copies[name] = remote(src, dst, sums_send.at[k, index], sums_recv.at[k, index], tensor=device)

        for place in range(4):
            add(("mate", place), sums_stage.at[k, place, 1 - core], sums_mate.at[k, place], mate)
        for q, part in enumerate(quarters):
            device, place, side = (right, RIGHT, 0) if q < 2 else (left, LEFT, 1)
            add((FAR, q), sums_out.at[k, FAR, part], sums_hop.at[k, q], device)
            add((place, q), sums_out.at[k, place, part], sums_final.at[k, side, part], device)
        for place, side, device, part in ((RIGHT, 0, right, halves[1]), (LEFT, 1, left, halves[0])):
            add((place, "half"), sums_out.at[k, place, part], sums_final.at[k, side, part], device)
        return copies

    sums = [sums_copies(0), sums_copies(1)]

    def chip_sum(k, place, part=slice(None)):
        return sums_stage[k, place, core, part].astype(F32) + sums_mate[k, place, part].astype(F32)

    def sums_first(k):
        sums[k]["mate", FAR].wait_recv()
        for q in (0, 2, 1, 3):
            sums_out[k, FAR, quarters[q]] = chip_sum(k, FAR, quarters[q]).astype(BF16)
            sums[k][FAR, q].start()

    def sums_second(k):
        for place, part in ((RIGHT, halves[1]), (LEFT, halves[0])):
            sums[k]["mate", place].wait_recv()
            sums_out[k, place, part] = chip_sum(k, place, part).astype(BF16)
            sums[k][place, "half"].start()

    def sums_third(k):
        for q in (0, 2, 1, 3):
            place, part = RIGHT if q < 2 else LEFT, quarters[q]
            sums[k][FAR, q].wait_recv()
            sums_out[k, place, part] = (chip_sum(k, place, part) + sums_hop[k, q].astype(F32)).astype(BF16)
            sums[k][place, q].start()

    def sums_last(k, write):
        sums[k]["mate", OWN].wait_recv()
        sums[k][RIGHT, "half"].wait_recv()
        sums[k][LEFT, "half"].wait_recv()
        for q in (0, 2, 1, 3):
            part = quarters[q]
            sums[k][RIGHT if q < 2 else LEFT, q].wait_recv()
            write(
                q,
                chip_sum(k, OWN, part)
                + sums_final[k, 0, part].astype(F32)
                + sums_final[k, 1, part].astype(F32),
            )

    def side_by_side(stacked):
        return jnp.concatenate([stacked[r] for r in head_rows], axis=1)

    wide_pick = jnp.broadcast_to(is_image, (rows, depth))
    attended_parts = by_expert(side_by_side(attended.astype(F32)), wide_pick, 1)

    def out_project(place):
        span = chip_of(places[place])
        block = dot(attended_parts[:, :depth], output_w[0, :, span]) + dot(
            attended_parts[:, depth:], output_w[1, :, span]
        )
        sums_stage[0, place] = block.T.astype(BF16).reshape(2, width, rows)
        sums[0]["mate", place].start()

    out_project(FAR)
    offset = jnp.sum(back_attended.astype(F32) * attended.astype(F32), axis=1, keepdims=True)

    outgoing = [("pair", turn, lax.rem(pair + turn, seq_size)) for turn in turns]
    outgoing += [("own", turn, lax.rem(seq + turn, seq_size)) for turn in turns]
    outgoing += [("pair", 0, pair), ("own", 0, seq)]
    mate_copies, back_copies = {}, {}
    for index, (name, turn, block) in enumerate(outgoing):
        mate_copies[index] = remote(
            memory_back.at[1 - core, block],
            memory_mate.at[index],
            mate_send.at[index],
            mate_recv.at[index],
            tensor=mate,
        )
        target = lax.rem(seq + turn, seq_size)
        if turn > 0 or name == "pair":
            back_copies[name, turn] = remote(
                memory_out.at[index],
                memory_in.at[index],
                back_send.at[index],
                back_recv.at[index],
                seq=target if turn > 0 else pair,
            )
    in_slot = {(name, turn): index for index, (name, turn, _) in enumerate(outgoing)}
    probability = (weights.astype(F32) / denominator).astype(BF16)
    back_probability = dot_nt(back_attended, values)
    back_score = (probability.astype(F32) * (back_probability - offset)).astype(BF16)
    memory_back[0] = (dot_tn(back_score, query_normed) * scale).astype(BF16).reshape(seq_size, rows, HEAD_DIM)
    memory_back[1] = dot_tn(probability, back_attended).astype(BF16).reshape(seq_size, rows, HEAD_DIM)
    for copy in mate_copies.values():
        copy.start()

    sums_first(0)
    out_project(RIGHT)

    kept = {}
    for index, (name, turn, block) in enumerate(outgoing):
        mate_copies[index].wait_recv()
        both = memory_back[core, block].astype(F32) + memory_mate[index].astype(F32)
        if turn > 0:
            memory_out[index] = both.astype(BF16)
            back_copies[name, turn].start()
        else:
            kept[name] = both

    out_project(LEFT)
    out_project(OWN)
    sums_second(0)

    back_query = dot(back_score, keys)
    query_factor = head_factor(query_raw)
    query_unit = query_raw * query_factor
    weighted = query_gain * (back_query * scale)
    query_back = query_factor * (
        weighted - query_unit * jnp.mean(weighted * query_unit, axis=-1, keepdims=True)
    )
    query_back = query_back.astype(BF16).astype(F32)
    inner = jnp.sum(side_by_side(query_back * query_raw), axis=1, keepdims=True)
    back_columns = jnp.concatenate([query_back[r].T for r in head_rows], axis=0)
    query_parts = by_expert(back_columns, jnp.concatenate([image_pick_t] * heads, axis=0), 0)
    for place in (FAR, RIGHT, LEFT, OWN):
        span = chip_of(places[place])
        partial_buf[place] = dot(query_w[0, span, :], query_parts[:depth]) + dot(
            query_w[1, span, :], query_parts[depth:]
        )

    def received(name):
        total = kept[name]
        for turn in turns:
            back_copies[name, turn].wait_recv()
            total = total + memory_in[in_slot[name, turn]].astype(F32)
        return total

    memory_out[in_slot["pair", 0]] = received("pair").astype(BF16)
    back_copies["pair", 0].start()
    sums_third(0)
    slice_grad = received("own")
    back_copies["pair", 0].wait_recv()
    slice_grad = slice_grad + memory_in[in_slot["pair", 0]].astype(F32)
    key_raw = key_raw_buf[...]
    key_factor = head_factor(key_raw)
    key_unit = key_raw * key_factor
    weighted = head_gain(1) * slice_grad
    key_back = key_factor * (weighted - key_unit * jnp.mean(weighted * key_unit, axis=-1, keepdims=True))
    slice_back = jnp.where(core == 0, key_back, slice_grad).astype(BF16).astype(F32)
    slice_parts = by_expert(slice_back.T, image_pick_t, 0)

    inner = inner + jnp.sum(slice_back * key_raw, axis=1, keepdims=True)
    inner_row = as_row(inner)
    inner_out[...] = jnp.broadcast_to(inner_row, inner_out.shape)
    inner_sends = {}
    for step in range(1, tensor_size):
        inner_sends[step] = remote(
            inner_out,
            inner_in.at[step],
            inner_send.at[step],
            inner_recv.at[step],
            tensor=lax.rem(me + step, tensor_size),
        )
        inner_sends[step].start()

    def key_project(place, parity):
        slot = places[place] - core + parity
        part = pl.ds(pl.multiple_of(parity * width, 64), width)
        total = (
            partial_buf[place, part, :]
            + dot(key_w[0, shard_of(slot), :], slice_parts[:HEAD_DIM])
            + dot(key_w[1, shard_of(slot), :], slice_parts[HEAD_DIM:])
        )
        sums_stage[1, place, parity] = total.astype(BF16)

    for place in (FAR, RIGHT, LEFT):
        key_project(place, 1 - core)
        sums[1]["mate", place].start()
        if place == FAR:
            key_project(place, core)
    key_project(OWN, 1 - core)
    sums[1]["mate", OWN].start()
    sums_first(1)
    key_project(RIGHT, core)
    key_project(LEFT, core)
    sums_second(1)
    key_project(OWN, core)

    def write_attention(q, total):
        attention_ref[quarters[q], :] = total.astype(BF16)

    sums_last(0, write_attention)
    sums_third(1)
    for step in range(1, tensor_size):
        inner_sends[step].wait_recv()
        inner_row = inner_row + inner_in[step, 0:1, :]
    inner_mean = inner_row / total_width

    def write_grad(q, total):
        here = shard_of(me, q * quarter, quarter)
        shift = rows_buf[0, here, :].astype(F32) * (factor_row * inner_mean)
        grad_ref[quarters[q], :] = (factor_row * (gain_buf[here, :] * total - shift)).astype(BF16)

    sums_last(1, write_grad)

    for copies in (*gathers, *sums, memory_copies, mate_copies, back_copies, inner_sends):
        for copy in copies.values():
            copy.wait_send()


def finish(attention_in, grad_in, attention_ref, grad_ref):
    attention_ref[...] = attention_in[...]
    grad_ref[...] = grad_in[...]


def solution(mesh):
    seq_size, tensor_size = mesh.shape["seq"], mesh.shape["tensor"]

    def local(
        inputs,
        cotangent,
        norm_gain,
        head_gain,
        query_weight,
        key_weight,
        output_weight,
        modality,
        segments,
        block_order,
    ):
        rows, width = inputs.shape
        total_width = width * tensor_size
        heads = query_weight.shape[2] // HEAD_DIM
        vmem = pl.BlockSpec(memory_space=pltpu.VMEM)
        anywhere = pl.BlockSpec(memory_space=pl.ANY)
        dma = pltpu.SemaphoreType.DMA
        shape = jax.ShapeDtypeStruct((width, rows), BF16)
        block = (seq_size, rows, HEAD_DIM)
        attention_out, grad_input = pl.pallas_call(
            functools.partial(kernel, seq_size, tensor_size),
            out_shape=(pltpu.VMEM((width, rows), BF16), pltpu.VMEM((width, rows), BF16)),
            in_specs=[anywhere] * 10,
            out_specs=(vmem, vmem),
            scratch_shapes=[
                pltpu.SMEM(block_order.shape, jnp.int32),
                pltpu.VMEM((1, rows), jnp.int32),
                pltpu.VMEM((seq_size, rows), jnp.int32),
                pltpu.VMEM(norm_gain.shape, F32),
                pltpu.VMEM(head_gain.shape, F32),
                pltpu.VMEM(query_weight.shape, BF16),
                pltpu.VMEM(key_weight.shape, BF16),
                pltpu.VMEM(output_weight.shape, BF16),
                pltpu.VMEM((2, total_width, rows), BF16),
                pltpu.VMEM((total_width, rows), F32),
                pltpu.VMEM((2, rows, heads * HEAD_DIM), F32),
                pltpu.VMEM((2, rows, HEAD_DIM), F32),
                pltpu.VMEM((2, heads * HEAD_DIM, rows), F32),
                pltpu.VMEM((heads * rows, HEAD_DIM), F32),
                pltpu.VMEM((rows, HEAD_DIM), F32),
                pltpu.VMEM((2, *block), BF16),
                pltpu.VMEM((heads * rows, HEAD_DIM), BF16),
                pltpu.VMEM((2, 4, 2, width, rows), BF16),
                pltpu.VMEM((2, 4, width, rows), BF16),
                pltpu.VMEM((2, 4, width // 4, rows), BF16),
                pltpu.VMEM((2, 3, width, rows), BF16),
                pltpu.VMEM((2, 2, width, rows), BF16),
                pltpu.VMEM((2, *block), BF16),
                pltpu.VMEM(block, BF16),
                pltpu.VMEM(block, BF16),
                pltpu.VMEM(block, BF16),
                pltpu.VMEM((4, 2 * width, rows), F32),
                pltpu.VMEM((8, rows), F32),
                pltpu.VMEM((tensor_size, 8, rows), F32),
                dma((10,)),
                dma((2, 21)),
                dma((2, 21)),
                dma((2 * seq_size,)),
                dma((2 * seq_size,)),
                dma((2, 14)),
                dma((2, 14)),
                dma((seq_size,)),
                dma((seq_size,)),
                dma((seq_size,)),
                dma((seq_size,)),
                dma((tensor_size,)),
                dma((tensor_size,)),
            ],
            compiler_params=pltpu.CompilerParams(collective_id=0, has_side_effects=True),
        )(
            block_order,
            modality.reshape(1, rows),
            segments.reshape(seq_size, rows),
            norm_gain,
            head_gain,
            inputs.T,
            cotangent.T,
            query_weight,
            key_weight,
            output_weight,
        )
        attention_out, grad_input = pl.pallas_call(
            finish,
            out_shape=(shape, shape),
            in_specs=[vmem, vmem],
            out_specs=(vmem, vmem),
            compiler_params=pltpu.CompilerParams(vmem_limit_bytes=2 << 20),
        )(attention_out, grad_input)
        return attention_out.T, grad_input.T

    return jax.shard_map(
        local,
        mesh=mesh,
        in_specs=(
            P(("dp", "seq"), "tensor"),
            P(("dp", "seq"), "tensor"),
            P(),
            P(),
            P(None, None, "tensor"),
            P(None, None, "tensor"),
            P(None, "tensor", None),
            P(("dp", "seq")),
            P("dp"),
            P("dp"),
        ),
        out_specs=(P(("dp", "seq"), "tensor"), P(("dp", "seq"), "tensor")),
        check_vma=False,
    )
```
